32 devices in a mesh: groups: 2 (over x), lon: 16 (over z, y, core).
Axes of the slice: x: 2, y: 2, z: 4, core: 2. Of those that a mesh axis runs over, the one named last changes fastest.
Arguments:
- white_noise: float32 [32, 256, 1024], P('groups', 'lon'), parts along dimension 0, may hold values from -6 to 6
- kappa_sq: float32 [256, 1024], P('lon'), may hold values from 0.05 to 1
- station_lat: float32 [16384], P(('groups', 'lon')), parts along dimension 0, may hold values from 0 to 1024
- station_lon: float32 [16384], P(('groups', 'lon')), parts along dimension 0, may hold values from 0 to 16
- station_weights: float32 [32, 8192], P('groups', 'lon'), parts along dimension 0, may hold values from -6 to 6
- station_count: int32 [32], P(('groups', 'lon')), parts along dimension 0, may hold values from 32 to 512, as said below
Outputs:
- posterior: float32 [32, 256, 1024], P('groups', 'lon'), parts along dimension 0
The draws below stay inside these ranges and needn't reach their ends.
There are 2 independent parts, one for each index of `groups`. The reference program is written for one: setup_inputs(seed, part) draws one part's arguments, and reference() takes and returns one part's arrays. A program takes and returns all parts, laid end to end along the dimension named above; an argument that names none is the same for every part. Nothing has to cross between parts.
Inputs may be any that keep to these rules, and one draw needn't show every extreme that they name: `station_count`: each tile's live stations fill its first slots; at least one tile has all 512 slots live.
All inputs are finite; a program needn't handle non-finite values.
Results may differ from the reference program's by a relative error of at most 0.0003.
Values sent between devices are 32-bit elements; how exact they have to be, the bound alone decides.
No kernel may reach another device: no remote copies, remote signals or barrier semaphores. Data moves between devices by JAX's collectives and lax.ppermute only.
A program may use at most 64 MiB of HBM per device.

```python
import math
import jax
import jax.numpy as jnp
from jax import lax

SAMPLES = 16
LAT = 1024
LON_DEV = 16
SLOTS = 512
PASSES = 8
HOPS = 2
TILES = 16
NLON = 256
STATIONS = 8192
RANGE = 32
N_LON = 16


def draw_station_count(key, part):
    first, second, third = jax.random.split(jax.random.fold_in(key, 7), 3)
    level = jax.random.randint(first, (TILES,), 0, 4)
    top = jnp.right_shift(jnp.int32(SLOTS), level)
    cut = jax.random.randint(second, (TILES,), 0, 1024) * (top // 2) // 1024
    counts = top - cut
    fullest = jax.random.randint(third, (), 0, TILES)
    return jnp.where(jnp.arange(TILES) == fullest, jnp.int32(SLOTS), counts).astype(jnp.int32)


def levels(rng, shape, shards, low, high):
    factor_of, own = 1.0, jax.random.fold_in(rng, 6)
    for dim, parts in shards:
        draws = jnp.exp(jax.random.uniform(jax.random.fold_in(own, dim), (parts,), jnp.float32, low / len(shards), high / len(shards)))
        factor_of = factor_of * jnp.repeat(draws, shape[dim] // parts).reshape([-1 if axis == dim else 1 for axis in range(len(shape))])
    return factor_of


def centred(stream_key, shape, spread, bound, pieces=(), kind=jnp.bfloat16):
    result = jax.random.normal(stream_key, shape, jnp.float32) * spread
    if len(pieces) > 0:
        result = levels(stream_key, shape, pieces, -0.22, 0.18) * result
    return jnp.clip(result, min=-bound, max=bound).astype(kind)


def setup_inputs(seed: int = 0, part: int = 0) -> dict:
    arg_keys = jax.random.split(jax.random.key(seed), 7)
    own_keys = jax.random.split(jax.random.fold_in(arg_keys[6], part), 7)
    return {
        "white_noise": centred(own_keys[0], (SAMPLES, NLON, LAT), 1.0, 6.0, ((1, 16),), jnp.float32),
        "kappa_sq": jnp.clip(jnp.exp(math.log(1.0) - 2.9957323 * jax.random.uniform(arg_keys[1], (NLON, LAT), jnp.float32) ** levels(arg_keys[1], (NLON, LAT), ((0, 16),), -0.2, 0.2)), 0.05, 1.0),
        "station_lat": jnp.clip(1024.0 * jax.random.uniform(own_keys[2], (STATIONS,), jnp.float32) ** levels(own_keys[2], (STATIONS,), ((0, 16),), -0.2, 0.2), 0.0, 1024.0),
        "station_lon": jnp.clip(16.0 * jax.random.uniform(own_keys[3], (STATIONS,), jnp.float32) ** levels(own_keys[3], (STATIONS,), ((0, 16),), -0.2, 0.2), 0.0, 16.0),
        "station_weights": centred(own_keys[4], (SAMPLES, STATIONS), 1.0, 6.0, ((1, 16),), jnp.float32),
        "station_count": draw_station_count(jax.random.fold_in(jax.random.fold_in(arg_keys[6], part), 71), part),
    }


cheb_coeffs = (0.62, -0.41, 0.3, -0.22, 0.16, -0.115, 0.08, -0.055, 0.04)

def apply_operator(field, kappa_sq):
    east = jnp.roll(field, -1, axis=1)
    west = jnp.roll(field, 1, axis=1)
    padded = jnp.pad(field, ((0, 0), (0, 0), (1, 1)))
    beside = east + west
    beside = beside + padded[:, :, 2:] + padded[:, :, :-2]
    return ((kappa_sq + 4.0) * field - beside) / 4.5 - field

def tile_terms(tile_step, lat_rows, lon_rows, weights, count):
    cell_lat = lax.broadcasted_iota(jnp.float32, (LON_DEV, LAT), 1).reshape(-1)
    cell_lon = lax.broadcasted_iota(jnp.float32, (LON_DEV, LAT), 0).reshape(-1)
    radius = jnp.float32(RANGE)
    shifted = lon_rows + jnp.float32(tile_step * LON_DEV)
    delta_lat = lat_rows[:, None] - cell_lat[None, :]
    delta_lon = shifted[:, None] - cell_lon[None, :]
    dist = jnp.sqrt(delta_lat * delta_lat + delta_lon * delta_lon)
    ratio = dist / radius
    taper = jnp.maximum(1.0 - ratio, 0.0) ** 4 * (4.0 * ratio + 1.0)
    kern = jnp.exp(-dist / radius) * taper
    slot = lax.iota(jnp.int32, SLOTS)
    kern = jnp.where((slot < count)[:, None], kern, jnp.float32(0.0))
    return jnp.dot(weights, kern, precision=lax.Precision.HIGHEST, preferred_element_type=jnp.float32)

def reference(white_noise, kappa_sq, station_lat, station_lon, station_weights, station_count):
    previous = white_noise
    current = apply_operator(white_noise, kappa_sq)
    prior = cheb_coeffs[0] * previous + cheb_coeffs[1] * current
    for level in range(2, PASSES + 1):
        following = 2.0 * apply_operator(current, kappa_sq) - previous
        prior = prior + cheb_coeffs[level] * following
        previous, current = (current, following)

    def tile_update(tile):
        total = jnp.zeros((SAMPLES, LON_DEV * LAT), jnp.float32)
        for tile_step in range(-HOPS, HOPS + 1):
            source = ((tile + tile_step) % N_LON).astype(jnp.int32)
            start = (source * SLOTS).astype(jnp.int32)
            lat_rows = lax.dynamic_slice_in_dim(station_lat, start, SLOTS)
            lon_rows = lax.dynamic_slice_in_dim(station_lon, start, SLOTS)
            weights = lax.dynamic_slice_in_dim(station_weights, start, SLOTS, 1)
            count = lax.dynamic_slice_in_dim(station_count, source, 1)[0]
            total = total + tile_terms(tile_step, lat_rows, lon_rows, weights, count)
        return total
    updates = lax.map(tile_update, jnp.arange(N_LON, dtype=jnp.int32))
    updates = updates.reshape(N_LON, SAMPLES, LON_DEV, LAT).transpose(1, 0, 2, 3).reshape(SAMPLES, NLON, LAT)
    return prior + updates
```

```python
import math

import jax
import jax.numpy as jnp
import numpy as np
from jax import lax
from jax.experimental import pallas as pl
from jax.experimental.pallas import tpu as pltpu
from jax.sharding import PartitionSpec as P

PASSES = 8
HOPS = 2
CHEB = (0.62, -0.41, 0.3, -0.22, 0.16, -0.115, 0.08, -0.055, 0.04)
LOG2E = math.log2(math.e)
FAR = 4096.0
CH = 32
LANES = 128


def horner_coeffs():
    powers = np.polynomial.chebyshev.cheb2poly(np.array(CHEB))
    lead = powers[PASSES]
    inner = [float(powers[k] / lead * (-4.5) ** (PASSES - k)) for k in range(PASSES)]
    return inner, float(lead / 4.5**PASSES)


def split3(value):
    high = value.astype(jnp.bfloat16)
    rest = value - high.astype(jnp.float32)
    middle = rest.astype(jnp.bfloat16)
    low = (rest - middle.astype(jnp.float32)).astype(jnp.bfloat16)
    return high, middle, low


def station_kernel(
    p0, p1, p2, p3, p4, x_hbm, out_ref, xt_hbm,
    table_v, table_s, data, sorted_s, merged, wts, latb, dlon2, stage, sem_s, sem_x,
    *, samples, width, height, slots,
):
    packs = (p0, p1, p2, p3, p4)
    lists = len(packs)
    radius = float(HOPS * width)
    band = int(radius)
    bands = height // band
    rows_m = (bands + 1 + 7) // 8 * 8
    scale = LOG2E / radius
    groups = band * width // LANES
    per_group = LANES // band
    for column in range(width):
        pltpu.make_async_copy(x_hbm.at[:, column, :], xt_hbm.at[column], sem_x.at[column]).start()

    index_m = lax.broadcasted_iota(jnp.int32, (rows_m, slots), 0).astype(jnp.float32)
    equal, below, onehot = [], [], []
    for pack in packs:
        lat = pack[samples : samples + 1, :]
        bucket = jnp.minimum(jnp.floor(lat * (1.0 / radius)), float(bands - 1))
        bucket = jnp.where(lat > FAR * 0.5, float(bands), bucket)
        bucket = jnp.broadcast_to(bucket, (rows_m, slots))
        equal.append(jnp.where(bucket == index_m, 1.0, 0.0))
        below.append(jnp.where(bucket < index_m, 1.0, 0.0).astype(jnp.bfloat16))
    before = lax.broadcasted_iota(jnp.int32, (slots, slots), 0) < lax.broadcasted_iota(
        jnp.int32, (slots, slots), 1
    )
    before = jnp.where(before, 1.0, 0.0).astype(jnp.bfloat16)
    all_below = jnp.concatenate(below, axis=0)
    inside = jnp.dot(
        jnp.concatenate(equal, axis=0).astype(jnp.bfloat16), before, preferred_element_type=jnp.float32
    )
    base = jnp.dot(all_below, jnp.ones((slots, LANES), jnp.bfloat16), preferred_element_type=jnp.float32)
    counts = lax.dot_general(
        jnp.ones((8, slots), jnp.bfloat16), all_below, (((1,), (1,)), ((), ())),
        preferred_element_type=jnp.float32,
    )
    table_v[...] = counts.astype(jnp.int32)
    copy = pltpu.make_async_copy(table_v, table_s, sem_s)
    copy.start()
    ranks = []
    for index in range(lists):
        rows = slice(index * rows_m, (index + 1) * rows_m)
        start = base[rows]
        start = jnp.concatenate([start] * (slots // LANES), axis=1)
        ranks.append(jnp.sum(equal[index] * (inside[rows] + start), axis=0, keepdims=True))

    factor = 4.0 * math.exp(-1.0) / LOG2E**5
    for index, pack in enumerate(packs):
        weights = pack[0:samples, :] * factor
        w_high = weights.astype(jnp.bfloat16)
        w_low = (weights - w_high.astype(jnp.float32)).astype(jnp.bfloat16)
        lat = pack[samples : samples + 1, :]
        lon = pack[samples + 1 : samples + 2, :] + float((index - HOPS) * width)
        parts = split3(lat) + split3(lon)
        parts = [part.astype(jnp.float32) for part in parts]
        filler = jnp.zeros((LANES - 2 * samples - 6, slots), jnp.float32)
        block = jnp.concatenate(
            [w_high.astype(jnp.float32), w_low.astype(jnp.float32)] + parts + [filler], axis=0
        )
        data[index] = block.astype(jnp.bfloat16)

    copy.wait()

    row_p = lax.broadcasted_iota(jnp.int32, (LANES, slots), 0).astype(jnp.float32)
    for index in range(lists):
        live = table_s[0, index * rows_m + bands]

        def sort_block(block, carry, index=index):
            first = block * LANES
            pick = ranks[index] - first.astype(jnp.float32)
            pick = jnp.where(jnp.broadcast_to(pick, (LANES, slots)) == row_p, 1.0, 0.0)
            moved = lax.dot_general(
                pick.astype(jnp.bfloat16), data[index], (((1,), (1,)), ((), ())),
                preferred_element_type=jnp.float32,
            )
            sorted_s[pl.ds(pl.multiple_of(index * slots + first, LANES), LANES), :] = moved
            return carry

        lax.fori_loop(0, (live + LANES - 1) // LANES, sort_block, 0)

    step = 24

    def merge_band(m, position):
        for index in range(lists):
            begin = table_s[0, index * rows_m + m]
            size = table_s[0, index * rows_m + m + 1] - begin
            source = index * slots + begin
            merged[pl.ds(position, step), :] = sorted_s[pl.ds(source, step), :]

            def more(k, carry, source=source, position=position):
                merged[pl.ds(position + k * step, step), :] = sorted_s[pl.ds(source + k * step, step), :]
                return carry

            lax.fori_loop(1, (size + step - 1) // step, more, 0)
            position = position + size
        return position

    total = lax.fori_loop(0, bands, merge_band, jnp.int32(0))
    lane = lax.broadcasted_iota(jnp.int32, (CH, LANES), 1)
    merged[pl.ds(total, CH), :] = jnp.where(lane == 2 * samples, FAR, 0.0)

    lane_row = lax.broadcasted_iota(jnp.int32, (1, LANES), 1)
    cell_in = (lane_row % band).astype(jnp.float32)
    cell_lon = (lane_row // band).astype(jnp.float32)

    def prepare(chunk, carry):
        first = pl.multiple_of(chunk * CH, CH)
        rows = merged[pl.ds(first, CH), :]

        def spread(at):
            value = rows[:, at : at + 1] + rows[:, at + 1 : at + 2]
            return jnp.broadcast_to(value + rows[:, at + 2 : at + 3], (CH, LANES))

        latb[pl.ds(first, CH), :] = spread(2 * samples)
        lon = spread(2 * samples + 3)
        for group in range(groups):
            offset = (lon - (cell_lon + float(group * per_group))) * scale
            dlon2[pl.ds(first, CH), group * LANES : (group + 1) * LANES] = offset * offset + 1e-30
        turned = rows.T
        left = turned[0 : 2 * samples, :]
        right = jnp.concatenate([turned[0:samples, :], jnp.zeros((samples, CH), jnp.float32)], axis=0)
        wts[chunk] = jnp.concatenate([left, right], axis=1).astype(jnp.bfloat16)
        return carry

    lax.fori_loop(0, (total + CH - 1) // CH, prepare, 0)

    def reach_of(m):
        first = jnp.int32(0)
        for index in range(lists):
            first = first + table_s[0, index * rows_m + m]
        return first

    def eval_band(m, carry):
        low = reach_of(jnp.maximum(m - 1, 0)) // CH
        high = (reach_of(jnp.minimum(m + 2, bands)) + CH - 1) // CH
        cells = cell_in + (m * band).astype(jnp.float32)

        def eval_chunk(chunk, total_sum):
            first = pl.multiple_of(chunk * CH, CH)
            offset = (latb[pl.ds(first, CH), :] - cells) * scale
            offset = offset * offset
            kerns = []
            for group in range(groups):
                square = offset + dlon2[pl.ds(first, CH), group * LANES : (group + 1) * LANES]
                taper = jnp.maximum(LOG2E - square * lax.rsqrt(square), 0.0)
                twice = taper * taper
                kerns.append((twice * twice) * (1.25 * LOG2E - taper) * jnp.exp2(taper))
            kern = jnp.concatenate(kerns, axis=1)
            high_part = kern.astype(jnp.bfloat16)
            low_part = (kern - high_part.astype(jnp.float32)).astype(jnp.bfloat16)
            both = jnp.concatenate([high_part, low_part], axis=0)
            return total_sum + jnp.dot(wts[chunk], both, preferred_element_type=jnp.float32)

        result = lax.fori_loop(
            low, high, eval_chunk, jnp.zeros((2 * samples, groups * LANES), jnp.float32)
        )
        stage[m] = result[0:samples] + result[samples : 2 * samples]
        return carry

    lax.fori_loop(0, bands, eval_band, 0)

    part = lax.broadcasted_iota(jnp.int32, (samples, LANES), 1) // band

    def lay_out(block, carry):
        at = pl.multiple_of(block * LANES, LANES)
        for group in range(groups):
            pieces = [
                stage[block * per_group + j, :, group * LANES : (group + 1) * LANES]
                for j in range(per_group)
            ]
            bit = 1
            while bit < per_group:
                keep = (part & bit) == 0
                for j in range(per_group):
                    if j & bit == 0:
                        first, second = pieces[j], pieces[j | bit]
                        pieces[j] = jnp.where(keep, first, pltpu.roll(second, bit * band, 1))
                        pieces[j | bit] = jnp.where(keep, pltpu.roll(first, LANES - bit * band, 1), second)
                bit *= 2
            for j in range(per_group):
                out_ref[group * per_group + j, :, pl.ds(at, LANES)] = pieces[j]
        return carry

    lax.fori_loop(0, height // LANES, lay_out, 0)
    for column in range(width):
        pltpu.make_async_copy(x_hbm.at[:, column, :], xt_hbm.at[column], sem_x.at[column]).wait()


def prior_kernel(
    xt_hbm, left_hbm, right_hbm, kappa_hbm, upd_hbm, out_hbm,
    noise, kap, betas, upd, first_y, second_y, sem_in, sem_upd, sem_out, *, samples, width, height,
):
    halo = PASSES
    inner, outer = horner_coeffs()
    edge = halo * samples
    own = width * samples
    copies = [
        pltpu.make_async_copy(xt_hbm, noise.at[pl.ds(edge, own)], sem_in.at[0]),
        pltpu.make_async_copy(left_hbm.at[pl.ds(0, edge)], noise.at[pl.ds(0, edge)], sem_in.at[1]),
        pltpu.make_async_copy(right_hbm.at[pl.ds(0, edge)], noise.at[pl.ds(edge + own, edge)], sem_in.at[2]),
        pltpu.make_async_copy(kappa_hbm, kap.at[pl.ds(halo, width)], sem_in.at[3]),
        pltpu.make_async_copy(left_hbm.at[pl.ds(edge, halo)], kap.at[pl.ds(0, halo)], sem_in.at[4]),
        pltpu.make_async_copy(right_hbm.at[pl.ds(edge, halo)], kap.at[pl.ds(halo + width, halo)], sem_in.at[5]),
    ]
    for copy in copies:
        copy.start()
    upd_copy = pltpu.make_async_copy(upd_hbm, upd, sem_upd)
    upd_copy.start()
    for copy in copies:
        copy.wait()
    tiles = height // LANES
    lane = lax.broadcasted_iota(jnp.int32, (samples, LANES), 1)
    at_low = lane == 0
    at_high = lane == LANES - 1
    columns = width + 2 * halo
    for column in range(columns):
        betas[column * 8 : (column + 1) * 8, :] = jnp.broadcast_to(kap[column : column + 1, :] - 0.5, (8, height))
    source = noise
    for turn in range(PASSES):
        target = (first_y, second_y)[turn % 2]
        level = PASSES - 1 - turn
        last = turn == PASSES - 1
        if last:
            upd_copy.wait()

        def pair(step, carry, source=source, target=target, level=level, last=last, turn=turn):
            column = turn + 1 + 2 * step
            for t in range(2):
                row = pl.multiple_of((column + t) * samples, samples)
                center = [
                    source[pl.ds(row, samples), i * LANES : (i + 1) * LANES] for i in range(tiles)
                ]
                up = [pltpu.roll(value, 1, 1) for value in center]
                down = [pltpu.roll(value, LANES - 1, 1) for value in center]
                for i in range(tiles):
                    lanes = slice(i * LANES, (i + 1) * LANES)
                    north = jnp.where(at_low, up[i - 1] if i > 0 else 0.0, up[i])
                    south = jnp.where(at_high, down[i + 1] if i < tiles - 1 else 0.0, down[i])
                    beside = source[pl.ds(row + samples, samples), lanes]
                    beside = beside + source[pl.ds(row - samples, samples), lanes]
                    beside = beside + (north + south)
                    beta = betas[pl.ds(pl.multiple_of((column + t) * 8, 8), 8), lanes]
                    beta = jnp.concatenate([beta] * (samples // 8), axis=0)
                    value = beside - beta * center[i]
                    value = value + inner[level] * noise[pl.ds(row, samples), lanes]
                    if last:
                        place = pl.multiple_of(row - edge, samples)
                        value = outer * value + upd[pl.ds(place, samples), lanes]
                        target[pl.ds(row, samples), lanes] = value
                    else:
                        target[pl.ds(row, samples), lanes] = value
                if last:
                    pltpu.make_async_copy(
                        target.at[pl.ds(row, samples)], out_hbm.at[:, column + t - halo, :],
                        sem_out.at[column + t - halo],
                    ).start()
            return carry

        lax.fori_loop(0, (columns - 2 * (turn + 1)) // 2, pair, 0)
        source = target
    for column in range(width):
        pltpu.make_async_copy(
            source.at[pl.ds((column + halo) * samples, samples)], out_hbm.at[:, column, :], sem_out.at[column]
        ).wait()


def shift_to(value, axis, steps):
    count = lax.axis_size(axis)
    return lax.ppermute(value, axis, [(source, (source + steps) % count) for source in range(count)])


def local(white_noise, kappa_sq, station_lat, station_lon, station_weights, station_count):
    samples, width, height = white_noise.shape
    slots = station_lat.shape[0]
    halo = PASSES
    live = lax.iota(jnp.int32, slots) < station_count[0]
    lat = jnp.where(live, station_lat, FAR)
    pack = jnp.concatenate([station_weights, lat[None], station_lon[None]], axis=0)
    packs = []
    for step in range(-HOPS, HOPS + 1):
        packs.append(pack if step == 0 else shift_to(pack, "lon", -step))

    def edge(columns):
        part = jnp.swapaxes(white_noise[:, columns, :], 0, 1).reshape(halo * samples, height)
        return jnp.concatenate([part, kappa_sq[columns]], axis=0)

    left = shift_to(edge(slice(width - halo, width)), "lon", 1)
    right = shift_to(edge(slice(0, halo)), "lon", -1)

    lists = 2 * HOPS + 1
    band = HOPS * width
    bands = height // band
    rows_m = (bands + 1 + 7) // 8 * 8
    room = lists * slots + 2 * LANES
    anywhere = pl.BlockSpec(memory_space=pl.ANY)
    whole = pl.BlockSpec(memory_space=pltpu.VMEM)
    upd, xt = pl.pallas_call(
        lambda *refs: station_kernel(*refs, samples=samples, width=width, height=height, slots=slots),
        out_shape=(
            jax.ShapeDtypeStruct((width, samples, height), jnp.float32),
            jax.ShapeDtypeStruct((width, samples, height), jnp.float32),
        ),
        in_specs=[whole] * lists + [anywhere],
        out_specs=(whole, anywhere),
        scratch_shapes=[
            pltpu.VMEM((8, lists * rows_m), jnp.int32),
            pltpu.SMEM((8, lists * rows_m), jnp.int32),
            pltpu.VMEM((lists, LANES, slots), jnp.bfloat16),
            pltpu.VMEM((room, LANES), jnp.float32),
            pltpu.VMEM((room, LANES), jnp.float32),
            pltpu.VMEM((room // CH, 2 * samples, 2 * CH), jnp.bfloat16),
            pltpu.VMEM((room, LANES), jnp.float32),
            pltpu.VMEM((room, band * width), jnp.float32),
            pltpu.VMEM((bands, samples, band * width), jnp.float32),
            pltpu.SemaphoreType.DMA,
            pltpu.SemaphoreType.DMA((width,)),
        ],
        name="stations",
    )(*packs, white_noise)
    rows = (width + 2 * halo) * samples
    return pl.pallas_call(
        lambda *refs: prior_kernel(*refs, samples=samples, width=width, height=height),
        out_shape=jax.ShapeDtypeStruct((samples, width, height), jnp.float32),
        in_specs=[anywhere] * 5,
        out_specs=anywhere,
        scratch_shapes=[
            pltpu.VMEM((rows, height), jnp.float32),
            pltpu.VMEM((width + 2 * halo, height), jnp.float32),
            pltpu.VMEM(((width + 2 * halo) * 8, height), jnp.float32),
            pltpu.VMEM((width * samples, height), jnp.float32),
            pltpu.VMEM((rows, height), jnp.float32),
            pltpu.VMEM((rows, height), jnp.float32),
            pltpu.SemaphoreType.DMA((6,)),
            pltpu.SemaphoreType.DMA,
            pltpu.SemaphoreType.DMA((width,)),
        ],
        name="prior",
    )(
        xt.reshape(width * samples, height), left, right, kappa_sq, upd.reshape(width * samples, height)
    )


def solution(mesh):
    in_specs = (
        P("groups", "lon", None),
        P("lon", None),
        P(("groups", "lon")),
        P(("groups", "lon")),
        P("groups", "lon"),
        P(("groups", "lon")),
    )
    out_specs = P("groups", "lon", None)
    return jax.shard_map(local, mesh=mesh, in_specs=in_specs, out_specs=out_specs, check_vma=False)
```

```python
import math

import jax
import jax.numpy as jnp
import numpy as np
from jax import lax
from jax.experimental import pallas as pl
from jax.experimental.pallas import tpu as pltpu
from jax.sharding import PartitionSpec as P

PASSES = 8
HOPS = 2
CHEB = (0.62, -0.41, 0.3, -0.22, 0.16, -0.115, 0.08, -0.055, 0.04)
LOG2E = math.log2(math.e)
FAR = 4096.0
CH = 32
UNROLL = 8
LANES = 128
BLOCK = 128


def horner_coeffs():
    powers = np.polynomial.chebyshev.cheb2poly(np.array(CHEB))
    lead = powers[PASSES]
    inner = [float(powers[k] / lead * (-4.5) ** (PASSES - k)) for k in range(PASSES)]
    return inner, float(lead / 4.5**PASSES)


def split3(value):
    high = value.astype(jnp.bfloat16)
    rest = value - high.astype(jnp.float32)
    middle = rest.astype(jnp.bfloat16)
    low = (rest - middle.astype(jnp.float32)).astype(jnp.bfloat16)
    return high, middle, low


def station_kernel(
    p0, p1, p2, p3, p4, out_ref,
    table_v, table_s, data, sorted_s, merged, wts, latb, dlon2, stage, starts, sem_s,
    *, samples, width, height, slots,
):
    packs = (p0, p1, p2, p3, p4)
    lists = len(packs)
    radius = float(HOPS * width)
    band = int(radius)
    bands = height // band
    rows_m = (bands + 1 + 7) // 8 * 8
    scale = LOG2E / radius
    groups = band * width // LANES
    per_group = LANES // band
    index_m = lax.broadcasted_iota(jnp.int32, (rows_m, slots), 0).astype(jnp.float32)
    equal, below, onehot = [], [], []
    for pack in packs:
        lat = pack[samples : samples + 1, :]
        bucket = jnp.minimum(jnp.floor(lat * (1.0 / radius)), float(bands - 1))
        bucket = jnp.where(lat > FAR * 0.5, float(bands), bucket)
        bucket = jnp.broadcast_to(bucket, (rows_m, slots))
        equal.append(jnp.where(bucket == index_m, 1.0, 0.0))
        below.append(jnp.where(bucket < index_m, 1.0, 0.0).astype(jnp.bfloat16))
    before = lax.broadcasted_iota(jnp.int32, (slots, slots), 0) < lax.broadcasted_iota(
        jnp.int32, (slots, slots), 1
    )
    before = jnp.where(before, 1.0, 0.0).astype(jnp.bfloat16)
    all_below = jnp.concatenate(below, axis=0)
    inside = jnp.dot(
        jnp.concatenate(equal, axis=0).astype(jnp.bfloat16), before, preferred_element_type=jnp.float32
    )
    base = jnp.dot(all_below, jnp.ones((slots, LANES), jnp.bfloat16), preferred_element_type=jnp.float32)
    counts = lax.dot_general(
        jnp.ones((8, slots), jnp.bfloat16), all_below, (((1,), (1,)), ((), ())),
        preferred_element_type=jnp.float32,
    )
    table_v[...] = counts.astype(jnp.int32)
    copy = pltpu.make_async_copy(table_v, table_s, sem_s)
    copy.start()
    ranks = []
    for index in range(lists):
        rows = slice(index * rows_m, (index + 1) * rows_m)
        start = base[rows]
        start = jnp.concatenate([start] * (slots // LANES), axis=1)
        ranks.append(jnp.sum(equal[index] * (inside[rows] + start), axis=0, keepdims=True))

    factor = 4.0 * math.exp(-1.0) / LOG2E**5
    for index, pack in enumerate(packs):
        weights = pack[0:samples, :] * factor
        w_high = weights.astype(jnp.bfloat16)
        w_low = (weights - w_high.astype(jnp.float32)).astype(jnp.bfloat16)
        lat = pack[samples : samples + 1, :]
        lon = pack[samples + 1 : samples + 2, :] + float((index - HOPS) * width)
        parts = split3(lat) + split3(lon)
        parts = [part.astype(jnp.float32) for part in parts]
        filler = jnp.zeros((LANES - 2 * samples - 6, slots), jnp.float32)
        block = jnp.concatenate(
            [w_high.astype(jnp.float32), w_low.astype(jnp.float32)] + parts + [filler], axis=0
        )
        data[index] = block.astype(jnp.bfloat16)

    copy.wait()

    row_p = lax.broadcasted_iota(jnp.int32, (LANES, slots), 0).astype(jnp.float32)
    for index in range(lists):
        live = table_s[0, index * rows_m + bands]

        def sort_block(block, carry, index=index):
            first = block * LANES
            pick = ranks[index] - first.astype(jnp.float32)
            pick = jnp.where(jnp.broadcast_to(pick, (LANES, slots)) == row_p, 1.0, 0.0)
            moved = lax.dot_general(
                pick.astype(jnp.bfloat16), data[index], (((1,), (1,)), ((), ())),
                preferred_element_type=jnp.float32,
            )
            sorted_s[pl.ds(pl.multiple_of(index * slots + first, LANES), LANES), :] = moved
            return carry

        lax.fori_loop(0, (live + LANES - 1) // LANES, sort_block, 0)

    step = 32

    def merge_band(m, position):
        starts[m] = position
        begins, sizes, places = [], [], []
        for index in range(lists):
            begin = table_s[0, index * rows_m + m]
            sizes.append(table_s[0, index * rows_m + m + 1] - begin)
            begins.append(index * slots + begin)
            places.append(position)
            position = position + sizes[-1]
        for index in range(lists):
            merged[pl.ds(places[index], step), :] = sorted_s[pl.ds(begins[index], step), :]
        largest = sizes[0]
        for size in sizes[1:]:
            largest = jnp.maximum(largest, size)

        @pl.when(largest > step)
        def _():
            for index in range(lists):

                def more(k, carry, index=index):
                    rows = sorted_s[pl.ds(begins[index] + k * step, step), :]
                    merged[pl.ds(places[index] + k * step, step), :] = rows
                    return carry

                lax.fori_loop(0, (sizes[index] + step - 1) // step, more, 0)

        return position

    total = lax.fori_loop(0, bands, merge_band, jnp.int32(0))
    starts[bands] = total
    lane = lax.broadcasted_iota(jnp.int32, (BLOCK, LANES), 1)
    merged[pl.ds(total, BLOCK), :] = jnp.where(lane == 2 * samples, FAR, 0.0)

    lane_row = lax.broadcasted_iota(jnp.int32, (1, LANES), 1)
    cell_in = (lane_row % band).astype(jnp.float32)
    cell_lon = (lane_row // band).astype(jnp.float32)

    def prepare(block, carry):
        first = pl.multiple_of(block * BLOCK, BLOCK)
        rows = merged[pl.ds(first, BLOCK), :]
        sums = rows + pltpu.roll(rows, LANES - 1, 1) + pltpu.roll(rows, LANES - 2, 1)
        latb[pl.ds(first, BLOCK), :] = jnp.broadcast_to(sums[:, 2 * samples : 2 * samples + 1], (BLOCK, LANES))
        lon = jnp.broadcast_to(sums[:, 2 * samples + 3 : 2 * samples + 4], (BLOCK, LANES))
        for group in range(groups):
            offset = (lon - (cell_lon + float(group * per_group))) * scale
            dlon2[pl.ds(first, BLOCK), group * LANES : (group + 1) * LANES] = offset * offset + 1e-30
        turned = rows.T
        for k in range(BLOCK // CH):
            left = turned[0 : 2 * samples, k * CH : (k + 1) * CH]
            right = jnp.concatenate([left[0:samples], jnp.zeros((samples, CH), jnp.float32)], axis=0)
            both = jnp.concatenate([left, right], axis=1)
            wts[block * (BLOCK // CH) + k] = both.astype(jnp.bfloat16)
        return carry

    lax.fori_loop(0, total // BLOCK + 1, prepare, 0)

    def low_of(m):
        return starts[jnp.maximum(m - 1, 0)] // CH

    def high_of(m):
        return jnp.maximum((starts[jnp.minimum(m + 2, bands)] + CH - 1) // CH, low_of(m) + 1)

    items = lax.fori_loop(0, bands, lambda m, count: count + high_of(m) - low_of(m), jnp.int32(0))
    for m in range(bands + 1):
        stage[m] = jnp.zeros((samples, groups * LANES), jnp.float32)

    def eval_items(step, carry):
        m, chunk = carry
        for _ in range(UNROLL):
            first = pl.multiple_of(chunk * CH, CH)
            offset = (latb[pl.ds(first, CH), :] - (cell_in + (m * band).astype(jnp.float32))) * scale
            offset = offset * offset
            kerns = []
            for group in range(groups):
                square = offset + dlon2[pl.ds(first, CH), group * LANES : (group + 1) * LANES]
                taper = jnp.maximum(LOG2E - square * lax.rsqrt(square), 0.0)
                twice = taper * taper
                kerns.append((twice * twice) * (1.25 * LOG2E - taper) * jnp.exp2(taper))
            kern = jnp.concatenate(kerns, axis=1)
            high_part = kern.astype(jnp.bfloat16)
            low_part = (kern - high_part.astype(jnp.float32)).astype(jnp.bfloat16)
            both = jnp.concatenate([high_part, low_part], axis=0)
            result = jnp.dot(wts[chunk], both, preferred_element_type=jnp.float32)
            stage[m] += result[0:samples] + result[samples : 2 * samples]
            done = chunk + 1 >= high_of(m)
            after = jnp.minimum(m + 1, bands)
            chunk = jnp.where(done, low_of(after), chunk + 1)
            chunk = jnp.where(after == bands, jnp.where(done, 0, chunk), chunk)
            m = jnp.where(done, after, m)
        return m, chunk

    lax.fori_loop(0, (items + UNROLL - 1) // UNROLL, eval_items, (jnp.int32(0), low_of(jnp.int32(0))))

    part = lax.broadcasted_iota(jnp.int32, (samples, LANES), 1) // band

    def lay_out(block, carry):
        at = pl.multiple_of(block * LANES, LANES)
        for group in range(groups):
            pieces = [
                stage[block * per_group + j, :, group * LANES : (group + 1) * LANES]
                for j in range(per_group)
            ]
            bit = 1
            while bit < per_group:
                keep = (part & bit) == 0
                for j in range(per_group):
                    if j & bit == 0:
                        first, second = pieces[j], pieces[j | bit]
                        pieces[j] = jnp.where(keep, first, pltpu.roll(second, bit * band, 1))
                        pieces[j | bit] = jnp.where(keep, pltpu.roll(first, LANES - bit * band, 1), second)
                bit *= 2
            for j in range(per_group):
                out_ref[group * per_group + j, :, pl.ds(at, LANES)] = pieces[j]
        return carry

    lax.fori_loop(0, height // LANES, lay_out, 0)


def prior_kernel(
    x_hbm, left_hbm, right_hbm, kappa_hbm, upd_hbm, out_hbm,
    noise, kap, betas, upd, first_y, second_y, sem_in, sem_x, sem_upd, sem_out, *, samples, width, height,
):
    halo = PASSES
    inner, outer = horner_coeffs()
    edge = halo * samples
    own = width * samples
    copies = [
        pltpu.make_async_copy(left_hbm.at[pl.ds(0, edge)], noise.at[pl.ds(0, edge)], sem_in.at[1]),
        pltpu.make_async_copy(right_hbm.at[pl.ds(0, edge)], noise.at[pl.ds(edge + own, edge)], sem_in.at[2]),
        pltpu.make_async_copy(kappa_hbm, kap.at[pl.ds(halo, width)], sem_in.at[3]),
        pltpu.make_async_copy(left_hbm.at[pl.ds(edge, halo)], kap.at[pl.ds(0, halo)], sem_in.at[4]),
        pltpu.make_async_copy(right_hbm.at[pl.ds(edge, halo)], kap.at[pl.ds(halo + width, halo)], sem_in.at[5]),
    ]
    for column in range(width):
        place = noise.at[pl.ds(edge + column * samples, samples)]
        copies.append(pltpu.make_async_copy(x_hbm.at[:, column, :], place, sem_x.at[column]))
    for copy in copies:
        copy.start()
    upd_copy = pltpu.make_async_copy(upd_hbm, upd, sem_upd)
    upd_copy.start()
    for copy in copies:
        copy.wait()
    tiles = height // LANES
    lane = lax.broadcasted_iota(jnp.int32, (samples, LANES), 1)
    at_low = lane == 0
    at_high = lane == LANES - 1
    columns = width + 2 * halo
    for column in range(columns):
        betas[column * 8 : (column + 1) * 8, :] = jnp.broadcast_to(kap[column : column + 1, :] - 0.5, (8, height))
    source = noise
    for turn in range(PASSES):
        target = (first_y, second_y)[turn % 2]
        level = PASSES - 1 - turn
        last = turn == PASSES - 1
        if last:
            upd_copy.wait()

        def pair(step, carry, source=source, target=target, level=level, last=last, turn=turn):
            column = turn + 1 + 4 * step
            for t in range(4):
                row = pl.multiple_of((column + t) * samples, samples)
                center = [
                    source[pl.ds(row, samples), i * LANES : (i + 1) * LANES] for i in range(tiles)
                ]
                up = [pltpu.roll(value, 1, 1) for value in center]
                down = [pltpu.roll(value, LANES - 1, 1) for value in center]
                for i in range(tiles):
                    lanes = slice(i * LANES, (i + 1) * LANES)
                    north = jnp.where(at_low, up[i - 1] if i > 0 else 0.0, up[i])
                    south = jnp.where(at_high, down[i + 1] if i < tiles - 1 else 0.0, down[i])
                    beside = source[pl.ds(row + samples, samples), lanes]
                    beside = beside + source[pl.ds(row - samples, samples), lanes]
                    beside = beside + (north + south)
                    beta = betas[pl.ds(pl.multiple_of((column + t) * 8, 8), 8), lanes]
                    beta = jnp.concatenate([beta] * (samples // 8), axis=0)
                    value = beside - beta * center[i]
                    value = value + inner[level] * noise[pl.ds(row, samples), lanes]
                    if last:
                        place = pl.multiple_of(row - edge, samples)
                        value = outer * value + upd[pl.ds(place, samples), lanes]
                        target[pl.ds(row, samples), lanes] = value
                    else:
                        target[pl.ds(row, samples), lanes] = value
                if last:
                    pltpu.make_async_copy(
                        target.at[pl.ds(row, samples)], out_hbm.at[:, column + t - halo, :],
                        sem_out.at[column + t - halo],
                    ).start()
            return carry

        lax.fori_loop(0, (columns - 2 * (turn + 1) + 3) // 4, pair, 0)
        source = target
    for column in range(width):
        pltpu.make_async_copy(
            source.at[pl.ds((column + halo) * samples, samples)], out_hbm.at[:, column, :], sem_out.at[column]
        ).wait()


def shift_to(value, axis, steps):
    count = lax.axis_size(axis)
    return lax.ppermute(value, axis, [(source, (source + steps) % count) for source in range(count)])


def local(white_noise, kappa_sq, station_lat, station_lon, station_weights, station_count):
    samples, width, height = white_noise.shape
    slots = station_lat.shape[0]
    halo = PASSES
    live = lax.iota(jnp.int32, slots) < station_count[0]
    lat = jnp.where(live, station_lat, FAR)
    pack = jnp.concatenate([station_weights, lat[None], station_lon[None]], axis=0)
    packs = []
    for step in range(-HOPS, HOPS + 1):
        packs.append(pack if step == 0 else shift_to(pack, "lon", -step))

    def edge(columns):
        part = jnp.swapaxes(white_noise[:, columns, :], 0, 1).reshape(halo * samples, height)
        return jnp.concatenate([part, kappa_sq[columns]], axis=0)

    held, edges = lax.optimization_barrier(
        (packs, (edge(slice(width - halo, width)), edge(slice(0, halo))))
    )
    packs = held
    left = shift_to(edges[0], "lon", 1)
    right = shift_to(edges[1], "lon", -1)

    lists = 2 * HOPS + 1
    band = HOPS * width
    bands = height // band
    rows_m = (bands + 1 + 7) // 8 * 8
    room = lists * slots + 2 * LANES
    anywhere = pl.BlockSpec(memory_space=pl.ANY)
    whole = pl.BlockSpec(memory_space=pltpu.VMEM)
    upd = pl.pallas_call(
        lambda *refs: station_kernel(*refs, samples=samples, width=width, height=height, slots=slots),
        out_shape=jax.ShapeDtypeStruct((width, samples, height), jnp.float32),
        in_specs=[whole] * lists,
        out_specs=whole,
        scratch_shapes=[
            pltpu.VMEM((8, lists * rows_m), jnp.int32),
            pltpu.SMEM((8, lists * rows_m), jnp.int32),
            pltpu.VMEM((lists, LANES, slots), jnp.bfloat16),
            pltpu.VMEM((room, LANES), jnp.float32),
            pltpu.VMEM((room, LANES), jnp.float32),
            pltpu.VMEM((room // CH, 2 * samples, 2 * CH), jnp.bfloat16),
            pltpu.VMEM((room, LANES), jnp.float32),
            pltpu.VMEM((room, band * width), jnp.float32),
            pltpu.VMEM((bands + 1, samples, band * width), jnp.float32),
            pltpu.SMEM((bands + 1,), jnp.int32),
            pltpu.SemaphoreType.DMA,
        ],
        name="stations",
    )(*packs)
    rows = (width + 2 * halo + 2) * samples
    return pl.pallas_call(
        lambda *refs: prior_kernel(*refs, samples=samples, width=width, height=height),
        out_shape=jax.ShapeDtypeStruct((samples, width, height), jnp.float32),
        in_specs=[anywhere] * 5,
        out_specs=anywhere,
        scratch_shapes=[
            pltpu.VMEM((rows, height), jnp.float32),
            pltpu.VMEM((width + 2 * halo, height), jnp.float32),
            pltpu.VMEM(((width + 2 * halo + 2) * 8, height), jnp.float32),
            pltpu.VMEM((width * samples, height), jnp.float32),
            pltpu.VMEM((rows, height), jnp.float32),
            pltpu.VMEM((rows, height), jnp.float32),
            pltpu.SemaphoreType.DMA((6,)),
            pltpu.SemaphoreType.DMA((width,)),
            pltpu.SemaphoreType.DMA,
            pltpu.SemaphoreType.DMA((width,)),
        ],
        name="prior",
    )(
        white_noise, left, right, kappa_sq, upd.reshape(width * samples, height)
    )


def solution(mesh):
    in_specs = (
        P("groups", "lon", None),
        P("lon", None),
        P(("groups", "lon")),
        P(("groups", "lon")),
        P("groups", "lon"),
        P(("groups", "lon")),
    )
    out_specs = P("groups", "lon", None)
    return jax.shard_map(local, mesh=mesh, in_specs=in_specs, out_specs=out_specs, check_vma=False)
```

```python
import math

import jax
import jax.numpy as jnp
import numpy as np
from jax import lax
from jax.experimental import pallas as pl
from jax.experimental.pallas import tpu as pltpu
from jax.sharding import PartitionSpec as P

PASSES = 8
HOPS = 2
CHEB = (0.62, -0.41, 0.3, -0.22, 0.16, -0.115, 0.08, -0.055, 0.04)
LOG2E = math.log2(math.e)
FAR = 4096.0
CH = 32
UNROLL = 8
LANES = 128
BLOCK = 128
ROOM = 24 * 2**20
PAD = 8
WIDE = 4


def horner_coeffs():
    powers = np.polynomial.chebyshev.cheb2poly(np.array(CHEB))
    lead = powers[PASSES]
    inner = [float(powers[k] / lead * (-4.5) ** (PASSES - k)) for k in range(PASSES)]
    return inner, float(lead / 4.5**PASSES)


def split3(value):
    high = value.astype(jnp.bfloat16)
    rest = value - high.astype(jnp.float32)
    middle = rest.astype(jnp.bfloat16)
    low = (rest - middle.astype(jnp.float32)).astype(jnp.bfloat16)
    return high, middle, low


def station_kernel(
    p0, p1, p2, p3, p4, out_ref,
    table_v, table_s, data, sorted_s, merged, wts, latb, dlon2, stage, starts, sem_s,
    *, samples, width, height, slots,
):
    packs = (p0, p1, p2, p3, p4)
    lists = len(packs)
    radius = float(HOPS * width)
    band = int(radius)
    bands = height // band
    rows_m = (bands + 1 + 7) // 8 * 8
    scale = LOG2E / radius
    groups = band * width // LANES
    per_group = LANES // band
    index_m = lax.broadcasted_iota(jnp.int32, (rows_m, slots), 0).astype(jnp.float32)
    equal, below, onehot = [], [], []
    for pack in packs:
        lat = pack[samples : samples + 1, :]
        bucket = jnp.minimum(jnp.floor(lat * (1.0 / radius)), float(bands - 1))
        bucket = jnp.where(lat > FAR * 0.5, float(bands), bucket)
        bucket = jnp.broadcast_to(bucket, (rows_m, slots))
        equal.append(jnp.where(bucket == index_m, 1.0, 0.0))
        below.append(jnp.where(bucket < index_m, 1.0, 0.0).astype(jnp.bfloat16))
    before = lax.broadcasted_iota(jnp.int32, (slots, slots), 0) < lax.broadcasted_iota(
        jnp.int32, (slots, slots), 1
    )
    before = jnp.where(before, 1.0, 0.0).astype(jnp.bfloat16)
    all_below = jnp.concatenate(below, axis=0)
    inside = jnp.dot(
        jnp.concatenate(equal, axis=0).astype(jnp.bfloat16), before, preferred_element_type=jnp.float32
    )
    base = jnp.dot(all_below, jnp.ones((slots, LANES), jnp.bfloat16), preferred_element_type=jnp.float32)
    counts = lax.dot_general(
        jnp.ones((8, slots), jnp.bfloat16), all_below, (((1,), (1,)), ((), ())),
        preferred_element_type=jnp.float32,
    )
    table_v[...] = counts.astype(jnp.int32)
    copy = pltpu.make_async_copy(table_v, table_s, sem_s)
    copy.start()
    ranks = []
    for index in range(lists):
        rows = slice(index * rows_m, (index + 1) * rows_m)
        start = base[rows]
        start = jnp.concatenate([start] * (slots // LANES), axis=1)
        ranks.append(jnp.sum(equal[index] * (inside[rows] + start), axis=0, keepdims=True))

    factor = 4.0 * math.exp(-1.0) / LOG2E**5
    for index, pack in enumerate(packs):
        weights = pack[0:samples, :] * factor
        w_high = weights.astype(jnp.bfloat16)
        w_low = (weights - w_high.astype(jnp.float32)).astype(jnp.bfloat16)
        lat = pack[samples : samples + 1, :]
        lon = pack[samples + 1 : samples + 2, :] + float((index - HOPS) * width)
        parts = split3(lat) + split3(lon)
        parts = [part.astype(jnp.float32) for part in parts]
        filler = jnp.zeros((LANES - 2 * samples - 6, slots), jnp.float32)
        block = jnp.concatenate(
            [w_high.astype(jnp.float32), w_low.astype(jnp.float32)] + parts + [filler], axis=0
        )
        data[index] = block.astype(jnp.bfloat16)

    copy.wait()

    row_p = lax.broadcasted_iota(jnp.int32, (LANES, slots), 0).astype(jnp.float32)
    for index in range(lists):
        live = table_s[0, index * rows_m + bands]

        def sort_block(block, carry, index=index):
            first = block * LANES
            pick = ranks[index] - first.astype(jnp.float32)
            pick = jnp.where(jnp.broadcast_to(pick, (LANES, slots)) == row_p, 1.0, 0.0)
            moved = lax.dot_general(
                pick.astype(jnp.bfloat16), data[index], (((1,), (1,)), ((), ())),
                preferred_element_type=jnp.float32,
            )
            sorted_s[pl.ds(pl.multiple_of(index * slots + first, LANES), LANES), :] = moved
            return carry

        lax.fori_loop(0, (live + LANES - 1) // LANES, sort_block, 0)

    step = 32

    def merge_band(m, position):
        starts[m] = position
        begins, sizes, places = [], [], []
        for index in range(lists):
            begin = table_s[0, index * rows_m + m]
            sizes.append(table_s[0, index * rows_m + m + 1] - begin)
            begins.append(index * slots + begin)
            places.append(position)
            position = position + sizes[-1]
        for index in range(lists):
            merged[pl.ds(places[index], step), :] = sorted_s[pl.ds(begins[index], step), :]
        largest = sizes[0]
        for size in sizes[1:]:
            largest = jnp.maximum(largest, size)

        @pl.when(largest > step)
        def _():
            for index in range(lists):

                def more(k, carry, index=index):
                    rows = sorted_s[pl.ds(begins[index] + k * step, step), :]
                    merged[pl.ds(places[index] + k * step, step), :] = rows
                    return carry

                lax.fori_loop(0, (sizes[index] + step - 1) // step, more, 0)

        return position

    total = lax.fori_loop(0, bands, merge_band, jnp.int32(0))
    starts[bands] = total
    lane = lax.broadcasted_iota(jnp.int32, (BLOCK, LANES), 1)
    merged[pl.ds(total, BLOCK), :] = jnp.where(lane == 2 * samples, FAR, 0.0)

    lane_row = lax.broadcasted_iota(jnp.int32, (1, LANES), 1)
    cell_in = (lane_row % band).astype(jnp.float32)
    cell_lon = (lane_row // band).astype(jnp.float32)

    def prepare(block, carry):
        first = pl.multiple_of(block * BLOCK, BLOCK)
        rows = merged[pl.ds(first, BLOCK), :]
        sums = rows + pltpu.roll(rows, LANES - 1, 1) + pltpu.roll(rows, LANES - 2, 1)
        latb[pl.ds(first, BLOCK), :] = jnp.broadcast_to(sums[:, 2 * samples : 2 * samples + 1], (BLOCK, LANES))
        lon = jnp.broadcast_to(sums[:, 2 * samples + 3 : 2 * samples + 4], (BLOCK, LANES))
        for group in range(groups):
            offset = (lon - (cell_lon + float(group * per_group))) * scale
            dlon2[pl.ds(first, BLOCK), group * LANES : (group + 1) * LANES] = offset * offset + 1e-30
        turned = rows.T
        for k in range(BLOCK // CH):
            left = turned[0 : 2 * samples, k * CH : (k + 1) * CH]
            right = jnp.concatenate([left[0:samples], jnp.zeros((samples, CH), jnp.float32)], axis=0)
            both = jnp.concatenate([left, right], axis=1)
            wts[block * (BLOCK // CH) + k] = both.astype(jnp.bfloat16)
        return carry

    lax.fori_loop(0, total // BLOCK + 1, prepare, 0)

    def low_of(m):
        return starts[jnp.maximum(m - 1, 0)] // CH

    def high_of(m):
        return jnp.maximum((starts[jnp.minimum(m + 2, bands)] + CH - 1) // CH, low_of(m) + 1)

    items = lax.fori_loop(0, bands, lambda m, count: count + high_of(m) - low_of(m), jnp.int32(0))
    for m in range(bands + 1):
        stage[m] = jnp.zeros((samples, groups * LANES), jnp.float32)

    def eval_items(step, carry):
        m, chunk = carry
        for _ in range(UNROLL):
            first = pl.multiple_of(chunk * CH, CH)
            offset = (latb[pl.ds(first, CH), :] - (cell_in + (m * band).astype(jnp.float32))) * scale
            offset = offset * offset
            kerns = []
            for group in range(groups):
                square = offset + dlon2[pl.ds(first, CH), group * LANES : (group + 1) * LANES]
                taper = jnp.maximum(LOG2E - square * lax.rsqrt(square), 0.0)
                twice = taper * taper
                kerns.append((twice * twice) * (1.25 * LOG2E - taper) * jnp.exp2(taper))
            kern = jnp.concatenate(kerns, axis=1)
            high_part = kern.astype(jnp.bfloat16)
            low_part = (kern - high_part.astype(jnp.float32)).astype(jnp.bfloat16)
            both = jnp.concatenate([high_part, low_part], axis=0)
            result = jnp.dot(wts[chunk], both, preferred_element_type=jnp.float32)
            stage[m] += result[0:samples] + result[samples : 2 * samples]
            done = chunk + 1 >= high_of(m)
            after = jnp.minimum(m + 1, bands)
            chunk = jnp.where(done, low_of(after), chunk + 1)
            chunk = jnp.where(after == bands, jnp.where(done, 0, chunk), chunk)
            m = jnp.where(done, after, m)
        return m, chunk

    lax.fori_loop(0, (items + UNROLL - 1) // UNROLL, eval_items, (jnp.int32(0), low_of(jnp.int32(0))))

    part = lax.broadcasted_iota(jnp.int32, (samples, LANES), 1) // band

    def lay_out(block, carry):
        at = pl.multiple_of(block * LANES, LANES)
        for group in range(groups):
            pieces = [
                stage[block * per_group + j, :, group * LANES : (group + 1) * LANES]
                for j in range(per_group)
            ]
            bit = 1
            while bit < per_group:
                keep = (part & bit) == 0
                for j in range(per_group):
                    if j & bit == 0:
                        first, second = pieces[j], pieces[j | bit]
                        pieces[j] = jnp.where(keep, first, pltpu.roll(second, bit * band, 1))
                        pieces[j | bit] = jnp.where(keep, pltpu.roll(first, LANES - bit * band, 1), second)
                bit *= 2
            for j in range(per_group):
                out_ref[group * per_group + j, :, pl.ds(at, LANES)] = pieces[j]
        return carry

    lax.fori_loop(0, height // LANES, lay_out, 0)


def turn_kernel(
    x_hbm, kappa_hbm, low_ref, high_ref, beta_ref, noise, kap, sem_x, sem_k, *, samples, width, height
):
    segments = height // LANES
    tall = height * samples // LANES
    copies = [pltpu.make_async_copy(x_hbm.at[:, c, :], noise.at[c], sem_x.at[c]) for c in range(width)]
    copies.append(pltpu.make_async_copy(kappa_hbm, kap, sem_k))
    for copy in copies:
        copy.start()
    copies[-1].wait()
    for column in range(width):
        half = (low_ref, high_ref)[column // PASSES]
        for i in range(segments):
            piece = kap[column : column + 1, i * LANES : (i + 1) * LANES]
            half[column % PASSES, tall + i : tall + i + 1, :] = piece
        beta_ref[column] = spread_kappa(half.at[column % PASSES], tall, samples, segments)
    for column in range(width):
        copies[column].wait()
    for column in range(width):
        half = (low_ref, high_ref)[column // PASSES]
        pieces = [noise[column, :, i * LANES : (i + 1) * LANES] for i in range(segments)]
        half[column % PASSES, 0:tall, :] = jnp.concatenate(pieces, axis=0).T


def spread_kappa(ref, start, samples, segments):
    rows = [ref[start + i : start + i + 1, :] - 0.5 for i in range(segments)]
    rows = [jnp.broadcast_to(row, (samples, LANES)) for row in rows]
    return jnp.concatenate(rows, axis=0).T


def prior_kernel(
    left_ref, low_ref, high_ref, right_ref, beta_ref, upd, out_hbm,
    noise, betas, first_y, second_y, result, sem_out, *, samples, width, height,
):
    halo = PASSES
    inner, outer = horner_coeffs()
    segments = height // LANES
    tall = height * samples // LANES
    columns = width + 2 * halo
    lane = lax.broadcasted_iota(jnp.int32, (8, LANES), 1)
    inner_low = lane >= samples
    inner_high = lane < LANES - samples

    def rims(buffer, column, top, bottom):
        buffer[column, 0:PAD, :] = jnp.where(inner_low, pltpu.roll(bottom, samples, 1), 0.0)
        buffer[column, PAD + tall : 2 * PAD + tall, :] = jnp.where(
            inner_high, pltpu.roll(top, LANES - samples, 1), 0.0
        )

    def bring(column, carry):
        for k, ref in enumerate((left_ref, low_ref, high_ref, right_ref)):
            place = k * halo + column
            noise[place, PAD : PAD + tall, :] = ref[column, 0:tall, :]
            rims(noise, place, ref[column, 0:8, :], ref[column, tall - 8 : tall, :])
        betas[column] = spread_kappa(left_ref.at[column], tall, samples, segments)
        betas[column + halo] = beta_ref[column]
        betas[column + 2 * halo] = beta_ref[column + halo]
        betas[column + 3 * halo] = spread_kappa(right_ref.at[column], tall, samples, segments)
        return carry

    lax.fori_loop(0, halo, bring, 0)
    source = noise
    for turn in range(PASSES):
        target = (first_y, second_y)[turn % 2]
        level = PASSES - 1 - turn
        last = turn == PASSES - 1

        def sweep(step, carry, source=source, target=target, level=level, last=last, turn=turn):
            column = turn + 1 + WIDE * step
            saved = [[] for _ in range(WIDE)]
            for r in range(tall // 8):
                rows = slice(PAD + r * 8, PAD + r * 8 + 8)
                north = slice(PAD + r * 8 - 1, PAD + r * 8 + 7)
                south = slice(PAD + r * 8 + 1, PAD + r * 8 + 9)
                line = [source[column + t, rows, :] for t in range(-1, WIDE + 1)]
                for t in range(WIDE):
                    beside = source[column + t, north, :] + source[column + t, south, :]
                    beside = beside + (line[t] + line[t + 2])
                    value = beside - betas[column + t, r * 8 : r * 8 + 8, :] * line[t + 1]
                    value = value + inner[level] * noise[column + t, rows, :]
                    if last or r == 0 or r == tall // 8 - 1:
                        saved[t].append(value)
                    if not last:
                        target[column + t, rows, :] = value
            for t in range(WIDE):
                if not last:
                    rims(target, column + t, saved[t][0], saved[t][-1])
                    continue
                own = column + t - halo
                turned = jnp.concatenate(saved[t], axis=0).T
                for i in range(segments):
                    lanes = slice(i * LANES, (i + 1) * LANES)
                    value = outer * turned[i * samples : (i + 1) * samples, :] + upd[own, :, lanes]
                    result[own, :, lanes] = value
                pltpu.make_async_copy(result.at[own], out_hbm.at[:, own, :], sem_out.at[own]).start()
            return carry

        lax.fori_loop(0, (columns - 2 * (turn + 1) + WIDE - 1) // WIDE, sweep, 0)
        source = target
    for column in range(width):
        pltpu.make_async_copy(result.at[column], out_hbm.at[:, column, :], sem_out.at[column]).wait()


def shift_to(value, axis, steps):
    count = lax.axis_size(axis)
    return lax.ppermute(value, axis, [(source, (source + steps) % count) for source in range(count)])


def local(white_noise, kappa_sq, station_lat, station_lon, station_weights, station_count):
    samples, width, height = white_noise.shape
    slots = station_lat.shape[0]
    halo = PASSES
    live = lax.iota(jnp.int32, slots) < station_count[0]
    lat = jnp.where(live, station_lat, FAR)
    pack = jnp.concatenate([station_weights, lat[None], station_lon[None]], axis=0)
    later = lax.optimization_barrier((pack, white_noise, kappa_sq))
    pack = later[0]
    packs = []
    for step in range(-HOPS, HOPS + 1):
        packs.append(pack if step == 0 else shift_to(pack, "lon", -step))

    anywhere = pl.BlockSpec(memory_space=pl.ANY)
    whole = pl.BlockSpec(memory_space=pltpu.VMEM)
    segments = height // LANES
    tall = height * samples // LANES
    half = pltpu.VMEM((halo, tall + segments, LANES), jnp.float32)
    low, high, beta = pl.pallas_call(
        lambda *refs: turn_kernel(*refs, samples=samples, width=width, height=height),
        out_shape=(half, half, pltpu.VMEM((width, tall, LANES), jnp.float32)),
        in_specs=[anywhere, anywhere],
        out_specs=(whole, whole, whole),
        scratch_shapes=[
            pltpu.VMEM((width, samples, height), jnp.float32),
            pltpu.VMEM((width, height), jnp.float32),
            pltpu.SemaphoreType.DMA((width,)),
            pltpu.SemaphoreType.DMA,
        ],
        compiler_params=pltpu.CompilerParams(vmem_limit_bytes=ROOM),
        name="turn",
    )(*later[1:])
    left = shift_to(high, "lon", 1)
    right = shift_to(low, "lon", -1)
    packs = [pltpu.with_memory_space_constraint(item, pltpu.VMEM) for item in packs]

    lists = 2 * HOPS + 1
    band = HOPS * width
    bands = height // band
    rows_m = (bands + 1 + 7) // 8 * 8
    room = lists * slots + 2 * LANES
    upd = pl.pallas_call(
        lambda *refs: station_kernel(*refs, samples=samples, width=width, height=height, slots=slots),
        out_shape=pltpu.VMEM((width, samples, height), jnp.float32),
        in_specs=[whole] * lists,
        out_specs=whole,
        scratch_shapes=[
            pltpu.VMEM((8, lists * rows_m), jnp.int32),
            pltpu.SMEM((8, lists * rows_m), jnp.int32),
            pltpu.VMEM((lists, LANES, slots), jnp.bfloat16),
            pltpu.VMEM((room, LANES), jnp.float32),
            pltpu.VMEM((room, LANES), jnp.float32),
            pltpu.VMEM((room // CH, 2 * samples, 2 * CH), jnp.bfloat16),
            pltpu.VMEM((room, LANES), jnp.float32),
            pltpu.VMEM((room, band * width), jnp.float32),
            pltpu.VMEM((bands + 1, samples, band * width), jnp.float32),
            pltpu.SMEM((bands + 1,), jnp.int32),
            pltpu.SemaphoreType.DMA,
        ],
        compiler_params=pltpu.CompilerParams(vmem_limit_bytes=ROOM),
        cost_estimate=pl.CostEstimate(flops=10000000000, transcendentals=10**7, bytes_accessed=2 * 10**6),
        name="stations",
    )(*packs)
    columns = width + 2 * halo
    field = pltpu.VMEM((columns + 2, tall + 2 * PAD, LANES), jnp.float32)
    fields = [left, low, high, right, beta, upd]
    fields = [pltpu.with_memory_space_constraint(item, pltpu.VMEM) for item in fields]
    return pl.pallas_call(
        lambda *refs: prior_kernel(*refs, samples=samples, width=width, height=height),
        out_shape=jax.ShapeDtypeStruct((samples, width, height), jnp.float32),
        in_specs=[whole] * 6,
        out_specs=anywhere,
        scratch_shapes=[
            field,
            pltpu.VMEM((columns + 2, tall, LANES), jnp.float32),
            field,
            field,
            pltpu.VMEM((width, samples, height), jnp.float32),
            pltpu.SemaphoreType.DMA((width,)),
        ],
        compiler_params=pltpu.CompilerParams(vmem_limit_bytes=ROOM),
        name="prior",
    )(*fields)


def solution(mesh):
    in_specs = (
        P("groups", "lon", None),
        P("lon", None),
        P(("groups", "lon")),
        P(("groups", "lon")),
        P("groups", "lon"),
        P(("groups", "lon")),
    )
    out_specs = P("groups", "lon", None)
    return jax.shard_map(local, mesh=mesh, in_specs=in_specs, out_specs=out_specs, check_vma=False)
```

```python
import math

import jax
import jax.numpy as jnp
import numpy as np
from jax import lax
from jax.experimental import pallas as pl
from jax.experimental.pallas import tpu as pltpu
from jax.sharding import PartitionSpec as P

PASSES = 8
HOPS = 2
CHEB = (0.62, -0.41, 0.3, -0.22, 0.16, -0.115, 0.08, -0.055, 0.04)
LOG2E = math.log2(math.e)
FAR = 4096.0
CH = 32
UNROLL = 16
LANES = 128
BLOCK = 128
ROOM = 24 * 2**20
PAD = 8
WIDE = 8


def horner_coeffs():
    powers = np.polynomial.chebyshev.cheb2poly(np.array(CHEB))
    lead = powers[PASSES]
    inner = [float(powers[k] / lead * (-4.5) ** (PASSES - k)) for k in range(PASSES)]
    return inner, float(lead / 4.5**PASSES)


def split3(value):
    high = value.astype(jnp.bfloat16)
    rest = value - high.astype(jnp.float32)
    middle = rest.astype(jnp.bfloat16)
    low = (rest - middle.astype(jnp.float32)).astype(jnp.bfloat16)
    return high, middle, low


def station_kernel(
    p0, p1, p2, p3, p4, out_ref,
    table_v, table_s, data, sorted_s, merged, wts, latb, dlon2, stage, starts, sem_s,
    *, samples, width, height, slots,
):
    packs = (p0, p1, p2, p3, p4)
    lists = len(packs)
    radius = float(HOPS * width)
    band = int(radius)
    bands = height // band
    rows_m = (bands + 1 + 7) // 8 * 8
    scale = LOG2E / radius
    groups = band * width // LANES
    per_group = LANES // band
    index_m = lax.broadcasted_iota(jnp.int32, (rows_m, slots), 0).astype(jnp.float32)
    equal, below, onehot = [], [], []
    for pack in packs:
        lat = pack[samples : samples + 1, :]
        bucket = jnp.minimum(jnp.floor(lat * (1.0 / radius)), float(bands - 1))
        bucket = jnp.where(lat > FAR * 0.5, float(bands), bucket)
        bucket = jnp.broadcast_to(bucket, (rows_m, slots))
        equal.append(jnp.where(bucket == index_m, 1.0, 0.0))
        below.append(jnp.where(bucket < index_m, 1.0, 0.0).astype(jnp.bfloat16))
    before = lax.broadcasted_iota(jnp.int32, (slots, slots), 0) < lax.broadcasted_iota(
        jnp.int32, (slots, slots), 1
    )
    before = jnp.where(before, 1.0, 0.0).astype(jnp.bfloat16)
    all_below = jnp.concatenate(below, axis=0)
    inside = jnp.dot(
        jnp.concatenate(equal, axis=0).astype(jnp.bfloat16), before, preferred_element_type=jnp.float32
    )
    base = jnp.dot(all_below, jnp.ones((slots, LANES), jnp.bfloat16), preferred_element_type=jnp.float32)
    counts = lax.dot_general(
        jnp.ones((8, slots), jnp.bfloat16), all_below, (((1,), (1,)), ((), ())),
        preferred_element_type=jnp.float32,
    )
    table_v[...] = counts.astype(jnp.int32)
    copy = pltpu.make_async_copy(table_v, table_s, sem_s)
    copy.start()
    ranks = []
    for index in range(lists):
        rows = slice(index * rows_m, (index + 1) * rows_m)
        start = base[rows]
        start = jnp.concatenate([start] * (slots // LANES), axis=1)
        ranks.append(jnp.sum(equal[index] * (inside[rows] + start), axis=0, keepdims=True))

    factor = 4.0 * math.exp(-1.0) / LOG2E**5
    for index, pack in enumerate(packs):
        weights = pack[0:samples, :] * factor
        w_high = weights.astype(jnp.bfloat16)
        w_low = (weights - w_high.astype(jnp.float32)).astype(jnp.bfloat16)
        lat = pack[samples : samples + 1, :]
        lon = pack[samples + 1 : samples + 2, :] + float((index - HOPS) * width)
        parts = split3(lat) + split3(lon)
        parts = [part.astype(jnp.float32) for part in parts]
        filler = jnp.zeros((LANES - 2 * samples - 6, slots), jnp.float32)
        block = jnp.concatenate(
            [w_high.astype(jnp.float32), w_low.astype(jnp.float32)] + parts + [filler], axis=0
        )
        data[index] = block.astype(jnp.bfloat16)

    copy.wait()

    row_p = lax.broadcasted_iota(jnp.int32, (LANES, slots), 0).astype(jnp.float32)
    longest = table_s[0, bands]
    for index in range(1, lists):
        longest = jnp.maximum(longest, table_s[0, index * rows_m + bands])

    def sort_block(block, carry):
        first = block * LANES
        for index in range(lists):
            pick = ranks[index] - first.astype(jnp.float32)
            pick = jnp.where(jnp.broadcast_to(pick, (LANES, slots)) == row_p, 1.0, 0.0)
            moved = lax.dot_general(
                pick.astype(jnp.bfloat16), data[index], (((1,), (1,)), ((), ())),
                preferred_element_type=jnp.float32,
            )
            sorted_s[pl.ds(pl.multiple_of(index * slots + first, LANES), LANES), :] = moved
        return carry

    lax.fori_loop(0, (longest + LANES - 1) // LANES, sort_block, 0)

    step = 32

    def merge_band(m, position):
        starts[m] = position
        begins, sizes, places = [], [], []
        for index in range(lists):
            begin = table_s[0, index * rows_m + m]
            sizes.append(table_s[0, index * rows_m + m + 1] - begin)
            begins.append(index * slots + begin)
            places.append(position)
            position = position + sizes[-1]
        for index in range(lists):
            merged[pl.ds(places[index], step), :] = sorted_s[pl.ds(begins[index], step), :]
        largest = sizes[0]
        for size in sizes[1:]:
            largest = jnp.maximum(largest, size)

        @pl.when(largest > step)
        def _():
            for index in range(lists):

                def more(k, carry, index=index):
                    rows = sorted_s[pl.ds(begins[index] + k * step, step), :]
                    merged[pl.ds(places[index] + k * step, step), :] = rows
                    return carry

                lax.fori_loop(0, (sizes[index] + step - 1) // step, more, 0)

        return position

    total = lax.fori_loop(0, bands, merge_band, jnp.int32(0))
    starts[bands] = total
    lane = lax.broadcasted_iota(jnp.int32, (BLOCK, LANES), 1)
    merged[pl.ds(total, BLOCK), :] = jnp.where(lane == 2 * samples, FAR, 0.0)

    lane_row = lax.broadcasted_iota(jnp.int32, (1, LANES), 1)
    cell_in = (lane_row % band).astype(jnp.float32)
    cell_lon = (lane_row // band).astype(jnp.float32)

    def prepare_pair(pair, carry):
        for half in range(2):
            prepare(2 * pair + half)
        return carry

    def prepare(block):
        first = pl.multiple_of(block * BLOCK, BLOCK)
        rows = merged[pl.ds(first, BLOCK), :]
        sums = rows + pltpu.roll(rows, LANES - 1, 1) + pltpu.roll(rows, LANES - 2, 1)
        latb[pl.ds(first, BLOCK), :] = jnp.broadcast_to(sums[:, 2 * samples : 2 * samples + 1], (BLOCK, LANES))
        lon = jnp.broadcast_to(sums[:, 2 * samples + 3 : 2 * samples + 4], (BLOCK, LANES))
        for group in range(groups):
            offset = (lon - (cell_lon + float(group * per_group))) * scale
            dlon2[pl.ds(first, BLOCK), group * LANES : (group + 1) * LANES] = offset * offset + 1e-30
        turned = rows.T
        for k in range(BLOCK // CH):
            left = turned[0 : 2 * samples, k * CH : (k + 1) * CH]
            right = jnp.concatenate([left[0:samples], jnp.zeros((samples, CH), jnp.float32)], axis=0)
            both = jnp.concatenate([left, right], axis=1)
            wts[block * (BLOCK // CH) + k] = both.astype(jnp.bfloat16)

    lax.fori_loop(0, total // (2 * BLOCK) + 1, prepare_pair, 0)

    def low_of(m):
        return starts[jnp.maximum(m - 1, 0)] // CH

    def high_of(m):
        return jnp.maximum((starts[jnp.minimum(m + 2, bands)] + CH - 1) // CH, low_of(m) + 1)

    items = lax.fori_loop(0, bands, lambda m, count: count + high_of(m) - low_of(m), jnp.int32(0))
    for m in range(bands + 1):
        stage[m] = jnp.zeros((samples, groups * LANES), jnp.float32)

    def eval_items(step, carry):
        m, chunk = carry
        for _ in range(UNROLL):
            first = pl.multiple_of(chunk * CH, CH)
            offset = (latb[pl.ds(first, CH), :] - (cell_in + (m * band).astype(jnp.float32))) * scale
            offset = offset * offset
            kerns = []
            for group in range(groups):
                square = offset + dlon2[pl.ds(first, CH), group * LANES : (group + 1) * LANES]
                taper = jnp.maximum(LOG2E - square * lax.rsqrt(square), 0.0)
                twice = taper * taper
                kerns.append((twice * twice) * (1.25 * LOG2E - taper) * jnp.exp2(taper))
            kern = jnp.concatenate(kerns, axis=1)
            high_part = kern.astype(jnp.bfloat16)
            low_part = (kern - high_part.astype(jnp.float32)).astype(jnp.bfloat16)
            both = jnp.concatenate([high_part, low_part], axis=0)
            result = jnp.dot(wts[chunk], both, preferred_element_type=jnp.float32)
            stage[m] += result[0:samples] + result[samples : 2 * samples]
            done = chunk + 1 >= high_of(m)
            after = jnp.minimum(m + 1, bands)
            chunk = jnp.where(done, low_of(after), chunk + 1)
            chunk = jnp.where(after == bands, jnp.where(done, 0, chunk), chunk)
            m = jnp.where(done, after, m)
        return m, chunk

    lax.fori_loop(0, (items + UNROLL - 1) // UNROLL, eval_items, (jnp.int32(0), low_of(jnp.int32(0))))

    part = lax.broadcasted_iota(jnp.int32, (samples, LANES), 1) // band

    def lay_out(block, carry):
        at = pl.multiple_of(block * LANES, LANES)
        for group in range(groups):
            pieces = [
                stage[block * per_group + j, :, group * LANES : (group + 1) * LANES]
                for j in range(per_group)
            ]
            bit = 1
            while bit < per_group:
                keep = (part & bit) == 0
                for j in range(per_group):
                    if j & bit == 0:
                        first, second = pieces[j], pieces[j | bit]
                        pieces[j] = jnp.where(keep, first, pltpu.roll(second, bit * band, 1))
                        pieces[j | bit] = jnp.where(keep, pltpu.roll(first, LANES - bit * band, 1), second)
                bit *= 2
            for j in range(per_group):
                out_ref[group * per_group + j, :, pl.ds(at, LANES)] = pieces[j]
        return carry

    lax.fori_loop(0, height // LANES, lay_out, 0)


def turn_kernel(
    x_hbm, kappa_hbm, low_ref, high_ref, beta_ref, noise, kap, sem_x, sem_k, *, samples, width, height
):
    segments = height // LANES
    tall = height * samples // LANES
    copies = [pltpu.make_async_copy(x_hbm.at[:, c, :], noise.at[c], sem_x.at[c]) for c in range(width)]
    copies.append(pltpu.make_async_copy(kappa_hbm, kap, sem_k))
    for copy in copies:
        copy.start()
    copies[-1].wait()
    for column in range(width):
        half = (low_ref, high_ref)[column // PASSES]
        for i in range(segments):
            piece = kap[column : column + 1, i * LANES : (i + 1) * LANES]
            half[column % PASSES, tall + i : tall + i + 1, :] = piece
        beta_ref[column] = spread_kappa(half.at[column % PASSES], tall, samples, segments)
    for column in range(width):
        copies[column].wait()
    for column in range(width):
        half = (low_ref, high_ref)[column // PASSES]
        pieces = [noise[column, :, i * LANES : (i + 1) * LANES] for i in range(segments)]
        half[column % PASSES, 0:tall, :] = jnp.concatenate(pieces, axis=0).T


def spread_kappa(ref, start, samples, segments):
    rows = [ref[start + i : start + i + 1, :] - 0.5 for i in range(segments)]
    rows = [jnp.broadcast_to(row, (samples, LANES)) for row in rows]
    return jnp.concatenate(rows, axis=0).T


def prior_kernel(
    left_ref, low_ref, high_ref, right_ref, beta_ref, upd, out_hbm,
    noise, betas, first_y, second_y, result, sem_out, *, samples, width, height,
):
    halo = PASSES
    inner, outer = horner_coeffs()
    segments = height // LANES
    tall = height * samples // LANES
    columns = width + 2 * halo
    pitch = tall + 2 * PAD
    lane = lax.broadcasted_iota(jnp.int32, (8, LANES), 1)
    sub = lax.broadcasted_iota(jnp.int32, (8, LANES), 0)
    on_top, on_bottom = sub == 0, sub == 7
    inner_low = lane >= samples
    inner_high = lane < LANES - samples

    def at(base, offset):
        return pl.ds(pl.multiple_of(base + offset, 8), 8)

    def bring(column, carry):
        for k, ref in enumerate((left_ref, low_ref, high_ref, right_ref)):
            base = (k * halo + column) * pitch
            noise[pl.ds(pl.multiple_of(base + PAD, 8), tall), :] = ref[column, 0:tall, :]
        betas[column] = spread_kappa(left_ref.at[column], tall, samples, segments)
        betas[column + halo] = beta_ref[column]
        betas[column + 2 * halo] = beta_ref[column + halo]
        betas[column + 3 * halo] = spread_kappa(right_ref.at[column], tall, samples, segments)
        return carry

    lax.fori_loop(0, halo, bring, 0)
    source = noise
    for turn in range(PASSES):
        target = (first_y, second_y)[turn % 2]
        level = PASSES - 1 - turn
        last = turn == PASSES - 1

        def sweep(column, count, source=source, target=target, level=level, last=last):
            base = column * pitch
            saved = [[] for _ in range(count)]
            for r in range(tall // 8):
                row = PAD + r * 8
                line = [source[at(base, t * pitch + row), :] for t in range(-1, count + 1)]
                for t in range(count):
                    north = source[pl.ds(base + (t * pitch + row - 1), 8), :]
                    south = source[pl.ds(base + (t * pitch + row + 1), 8), :]
                    if r == 0:
                        end = source[pl.ds(base + (t * pitch + PAD + tall - 1), 8), :]
                        end = jnp.where(inner_low, pltpu.roll(end, samples, 1), 0.0)
                        north = jnp.where(on_top, end, north)
                    if r == tall // 8 - 1:
                        end = source[pl.ds(base + (t * pitch + PAD - 7), 8), :]
                        end = jnp.where(inner_high, pltpu.roll(end, LANES - samples, 1), 0.0)
                        south = jnp.where(on_bottom, end, south)
                    beside = (north + south) + (line[t] + line[t + 2])
                    value = beside - betas[column + t, r * 8 : r * 8 + 8, :] * line[t + 1]
                    value = value + inner[level] * noise[at(base, t * pitch + row), :]
                    if last:
                        saved[t].append(value)
                    else:
                        target[at(base, t * pitch + row), :] = value
            for t in range(count if last else 0):
                own = column + t - halo
                turned = jnp.concatenate(saved[t], axis=0).T
                for i in range(segments):
                    lanes = slice(i * LANES, (i + 1) * LANES)
                    value = outer * turned[i * samples : (i + 1) * samples, :] + upd[own, :, lanes]
                    result[own, :, lanes] = value
                pltpu.make_async_copy(result.at[own], out_hbm.at[:, own, :], sem_out.at[own]).start()

        def step_wide(step, carry, sweep=sweep, turn=turn):
            sweep(turn + 1 + WIDE * step, WIDE)
            return carry

        count = columns - 2 * (turn + 1)
        lax.fori_loop(0, count // WIDE, step_wide, 0)
        if count % WIDE:
            sweep(jnp.int32(turn + 1 + count - count % WIDE), count % WIDE)
        source = target
    for column in range(width):
        pltpu.make_async_copy(result.at[column], out_hbm.at[:, column, :], sem_out.at[column]).wait()


def shift_to(value, axis, steps):
    count = lax.axis_size(axis)
    return lax.ppermute(value, axis, [(source, (source + steps) % count) for source in range(count)])


def local(white_noise, kappa_sq, station_lat, station_lon, station_weights, station_count):
    samples, width, height = white_noise.shape
    slots = station_lat.shape[0]
    halo = PASSES
    live = lax.iota(jnp.int32, slots) < station_count[0]
    lat = jnp.where(live, station_lat, FAR)
    pack = jnp.concatenate([station_weights, lat[None], station_lon[None]], axis=0)
    later = lax.optimization_barrier((pack, white_noise, kappa_sq))
    pack = later[0]
    packs = []
    for step in range(-HOPS, HOPS + 1):
        packs.append(pack if step == 0 else shift_to(pack, "lon", -step))

    anywhere = pl.BlockSpec(memory_space=pl.ANY)
    whole = pl.BlockSpec(memory_space=pltpu.VMEM)
    segments = height // LANES
    tall = height * samples // LANES
    half = pltpu.VMEM((halo, tall + segments, LANES), jnp.float32)
    low, high, beta = pl.pallas_call(
        lambda *refs: turn_kernel(*refs, samples=samples, width=width, height=height),
        out_shape=(half, half, pltpu.VMEM((width, tall, LANES), jnp.float32)),
        in_specs=[pl.BlockSpec(memory_space=pltpu.HBM), pl.BlockSpec(memory_space=pltpu.HBM)],
        out_specs=(whole, whole, whole),
        scratch_shapes=[
            pltpu.VMEM((width, samples, height), jnp.float32),
            pltpu.VMEM((width, height), jnp.float32),
            pltpu.SemaphoreType.DMA((width,)),
            pltpu.SemaphoreType.DMA,
        ],
        compiler_params=pltpu.CompilerParams(vmem_limit_bytes=ROOM),
        name="turn",
    )(*[pltpu.with_memory_space_constraint(item, pltpu.HBM) for item in later[1:]])
    left = shift_to(high, "lon", 1)
    right = shift_to(low, "lon", -1)
    packs = [pltpu.with_memory_space_constraint(item, pltpu.VMEM) for item in packs]

    lists = 2 * HOPS + 1
    band = HOPS * width
    bands = height // band
    rows_m = (bands + 1 + 7) // 8 * 8
    room = lists * slots + 2 * LANES
    upd = pl.pallas_call(
        lambda *refs: station_kernel(*refs, samples=samples, width=width, height=height, slots=slots),
        out_shape=pltpu.VMEM((width, samples, height), jnp.float32),
        in_specs=[whole] * lists,
        out_specs=whole,
        scratch_shapes=[
            pltpu.VMEM((8, lists * rows_m), jnp.int32),
            pltpu.SMEM((8, lists * rows_m), jnp.int32),
            pltpu.VMEM((lists, LANES, slots), jnp.bfloat16),
            pltpu.VMEM((room, LANES), jnp.float32),
            pltpu.VMEM((room, LANES), jnp.float32),
            pltpu.VMEM((room // CH, 2 * samples, 2 * CH), jnp.bfloat16),
            pltpu.VMEM((room, LANES), jnp.float32),
            pltpu.VMEM((room, band * width), jnp.float32),
            pltpu.VMEM((bands + 1, samples, band * width), jnp.float32),
            pltpu.SMEM((bands + 1,), jnp.int32),
            pltpu.SemaphoreType.DMA,
        ],
        compiler_params=pltpu.CompilerParams(vmem_limit_bytes=ROOM),
        cost_estimate=pl.CostEstimate(flops=10000000000, transcendentals=10**7, bytes_accessed=2 * 10**6),
        name="stations",
    )(*packs)
    columns = width + 2 * halo
    field = pltpu.VMEM(((columns + 2) * (tall + 2 * PAD), LANES), jnp.float32)
    fields = [left, low, high, right, beta, upd]
    fields = [pltpu.with_memory_space_constraint(item, pltpu.VMEM) for item in fields]
    return pl.pallas_call(
        lambda *refs: prior_kernel(*refs, samples=samples, width=width, height=height),
        out_shape=jax.ShapeDtypeStruct((samples, width, height), jnp.float32),
        in_specs=[whole] * 6,
        out_specs=anywhere,
        scratch_shapes=[
            field,
            pltpu.VMEM((columns + 2, tall, LANES), jnp.float32),
            field,
            field,
            pltpu.VMEM((width, samples, height), jnp.float32),
            pltpu.SemaphoreType.DMA((width,)),
        ],
        compiler_params=pltpu.CompilerParams(vmem_limit_bytes=ROOM),
        name="prior",
    )(*fields)


def solution(mesh):
    in_specs = (
        P("groups", "lon", None),
        P("lon", None),
        P(("groups", "lon")),
        P(("groups", "lon")),
        P("groups", "lon"),
        P(("groups", "lon")),
    )
    out_specs = P("groups", "lon", None)
    return jax.shard_map(local, mesh=mesh, in_specs=in_specs, out_specs=out_specs, check_vma=False)
```

```python
import math

import jax
import jax.numpy as jnp
import numpy as np
from jax import lax
from jax.experimental import pallas as pl
from jax.experimental.pallas import tpu as pltpu
from jax.sharding import PartitionSpec as P

PASSES = 8
HOPS = 2
CHEB = (0.62, -0.41, 0.3, -0.22, 0.16, -0.115, 0.08, -0.055, 0.04)
LOG2E = math.log2(math.e)
FAR = 4096.0
CH = 32
UNROLL = 16
LANES = 128
BLOCK = 128
ROOM = 24 * 2**20
PAD = 8
WIDE = 8


def horner_coeffs():
    powers = np.polynomial.chebyshev.cheb2poly(np.array(CHEB))
    lead = powers[PASSES]
    inner = [float(powers[k] / lead * (-4.5) ** (PASSES - k)) for k in range(PASSES)]
    return inner, float(lead / 4.5**PASSES)


def split3(value):
    high = value.astype(jnp.bfloat16)
    rest = value - high.astype(jnp.float32)
    middle = rest.astype(jnp.bfloat16)
    low = (rest - middle.astype(jnp.float32)).astype(jnp.bfloat16)
    return high, middle, low


def station_kernel(
    p0, p1, p2, p3, p4, out_ref,
    table_v, table_s, data, sorted_s, merged, wts, latb, dlon2, stage, starts, sem_s,
    *, samples, width, height, slots,
):
    packs = (p0, p1, p2, p3, p4)
    lists = len(packs)
    radius = float(HOPS * width)
    band = int(radius)
    bands = height // band
    rows_m = (bands + 1 + 7) // 8 * 8
    scale = LOG2E / radius
    groups = band * width // LANES
    per_group = LANES // band
    index_m = lax.broadcasted_iota(jnp.int32, (rows_m, slots), 0).astype(jnp.float32)
    equal, below, onehot = [], [], []
    for pack in packs:
        lat = pack[samples : samples + 1, :]
        bucket = jnp.minimum(jnp.floor(lat * (1.0 / radius)), float(bands - 1))
        bucket = jnp.where(lat > FAR * 0.5, float(bands), bucket)
        bucket = jnp.broadcast_to(bucket, (rows_m, slots))
        equal.append(jnp.where(bucket == index_m, 1.0, 0.0))
        below.append(jnp.where(bucket < index_m, 1.0, 0.0).astype(jnp.bfloat16))
    before = lax.broadcasted_iota(jnp.int32, (slots, slots), 0) < lax.broadcasted_iota(
        jnp.int32, (slots, slots), 1
    )
    before = jnp.where(before, 1.0, 0.0).astype(jnp.bfloat16)
    all_below = jnp.concatenate(below, axis=0)
    inside = jnp.dot(
        jnp.concatenate(equal, axis=0).astype(jnp.bfloat16), before, preferred_element_type=jnp.float32
    )
    base = jnp.dot(all_below, jnp.ones((slots, LANES), jnp.bfloat16), preferred_element_type=jnp.float32)
    counts = lax.dot_general(
        jnp.ones((8, slots), jnp.bfloat16), all_below, (((1,), (1,)), ((), ())),
        preferred_element_type=jnp.float32,
    )
    table_v[...] = counts.astype(jnp.int32)
    copy = pltpu.make_async_copy(table_v, table_s, sem_s)
    copy.start()
    ranks = []
    for index in range(lists):
        rows = slice(index * rows_m, (index + 1) * rows_m)
        start = base[rows]
        start = jnp.concatenate([start] * (slots // LANES), axis=1)
        ranks.append(jnp.sum(equal[index] * (inside[rows] + start), axis=0, keepdims=True))

    factor = 4.0 * math.exp(-1.0) / LOG2E**5
    for index, pack in enumerate(packs):
        weights = pack[0:samples, :] * factor
        w_high = weights.astype(jnp.bfloat16)
        w_low = (weights - w_high.astype(jnp.float32)).astype(jnp.bfloat16)
        lat = pack[samples : samples + 1, :]
        lon = pack[samples + 1 : samples + 2, :] + float((index - HOPS) * width)
        parts = split3(lat) + split3(lon)
        parts = [part.astype(jnp.float32) for part in parts]
        filler = jnp.zeros((LANES - 2 * samples - 6, slots), jnp.float32)
        block = jnp.concatenate(
            [w_high.astype(jnp.float32), w_low.astype(jnp.float32)] + parts + [filler], axis=0
        )
        data[index] = block.astype(jnp.bfloat16)

    copy.wait()

    row_p = lax.broadcasted_iota(jnp.int32, (LANES, slots), 0).astype(jnp.float32)
    longest = table_s[0, bands]
    for index in range(1, lists):
        longest = jnp.maximum(longest, table_s[0, index * rows_m + bands])

    def sort_block(block, carry):
        first = block * LANES
        for index in range(lists):
            pick = ranks[index] - first.astype(jnp.float32)
            pick = jnp.where(jnp.broadcast_to(pick, (LANES, slots)) == row_p, 1.0, 0.0)
            moved = lax.dot_general(
                pick.astype(jnp.bfloat16), data[index], (((1,), (1,)), ((), ())),
                preferred_element_type=jnp.float32,
            )
            sorted_s[pl.ds(pl.multiple_of(index * slots + first, LANES), LANES), :] = moved
        return carry

    lax.fori_loop(0, (longest + LANES - 1) // LANES, sort_block, 0)

    step = 32

    def merge_band(m, position):
        starts[m] = position
        begins, sizes, places = [], [], []
        for index in range(lists):
            begin = table_s[0, index * rows_m + m]
            sizes.append(table_s[0, index * rows_m + m + 1] - begin)
            begins.append(index * slots + begin)
            places.append(position)
            position = position + sizes[-1]
        for index in range(lists):
            merged[pl.ds(places[index], step), :] = sorted_s[pl.ds(begins[index], step), :]
        largest = sizes[0]
        for size in sizes[1:]:
            largest = jnp.maximum(largest, size)

        @pl.when(largest > step)
        def _():
            for index in range(lists):

                def more(k, carry, index=index):
                    rows = sorted_s[pl.ds(begins[index] + k * step, step), :]
                    merged[pl.ds(places[index] + k * step, step), :] = rows
                    return carry

                lax.fori_loop(0, (sizes[index] + step - 1) // step, more, 0)

        return position

    total = lax.fori_loop(0, bands, merge_band, jnp.int32(0))
    starts[bands] = total
    lane = lax.broadcasted_iota(jnp.int32, (BLOCK, LANES), 1)
    merged[pl.ds(total, BLOCK), :] = jnp.where(lane == 2 * samples, FAR, 0.0)

    lane_row = lax.broadcasted_iota(jnp.int32, (1, LANES), 1)
    cell_in = (lane_row % band).astype(jnp.float32)
    cell_lon = (lane_row // band).astype(jnp.float32)

    row_of = lax.broadcasted_iota(jnp.int32, (LANES, 2 * LANES), 0) - 2 * samples
    part_of = lax.broadcasted_iota(jnp.int32, (LANES, 2 * LANES), 1) // LANES * 3
    gather = jnp.where((row_of >= part_of) & (row_of < part_of + 3), 1.0, 0.0).astype(jnp.bfloat16)
    turn_rows = lax.broadcasted_iota(jnp.int32, (2 * samples, LANES), 0)
    turn_lanes = lax.broadcasted_iota(jnp.int32, (2 * samples, LANES), 1)
    select = jnp.where(turn_rows == turn_lanes, 1.0, 0.0).astype(jnp.bfloat16)
    is_high = lax.broadcasted_iota(jnp.int32, (CH, LANES), 1) < samples

    def prepare_pair(pair, carry):
        for half in range(2):
            prepare(2 * pair + half)
        return carry

    def prepare(block):
        first = pl.multiple_of(block * BLOCK, BLOCK)
        rows = merged[pl.ds(first, BLOCK), :]
        places = jnp.dot(rows.astype(jnp.bfloat16), gather, preferred_element_type=jnp.float32)
        latb[pl.ds(first, BLOCK), :] = places[:, 0:LANES]
        lon = places[:, LANES : 2 * LANES]
        for group in range(groups):
            offset = (lon - (cell_lon + float(group * per_group))) * scale
            dlon2[pl.ds(first, BLOCK), group * LANES : (group + 1) * LANES] = offset * offset + 1e-30
        for k in range(BLOCK // CH):
            some = rows[k * CH : (k + 1) * CH, :]
            both = jnp.concatenate([some, jnp.where(is_high, some, 0.0)], axis=0).astype(jnp.bfloat16)
            turned = lax.dot_general(
                select, both, (((1,), (1,)), ((), ())), preferred_element_type=jnp.float32
            )
            wts[block * (BLOCK // CH) + k] = turned.astype(jnp.bfloat16)

    lax.fori_loop(0, total // (2 * BLOCK) + 1, prepare_pair, 0)

    def low_of(m):
        return starts[jnp.maximum(m - 1, 0)] // CH

    def high_of(m):
        return jnp.maximum((starts[jnp.minimum(m + 2, bands)] + CH - 1) // CH, low_of(m) + 1)

    items = lax.fori_loop(0, bands, lambda m, count: count + high_of(m) - low_of(m), jnp.int32(0))
    for m in range(bands + 1):
        stage[m] = jnp.zeros((samples, groups * LANES), jnp.float32)

    def eval_items(step, carry):
        m, chunk = carry
        for _ in range(UNROLL):
            first = pl.multiple_of(chunk * CH, CH)
            offset = (latb[pl.ds(first, CH), :] - (cell_in + (m * band).astype(jnp.float32))) * scale
            offset = offset * offset
            kerns = []
            for group in range(groups):
                square = offset + dlon2[pl.ds(first, CH), group * LANES : (group + 1) * LANES]
                taper = jnp.maximum(LOG2E - square * lax.rsqrt(square), 0.0)
                twice = taper * taper
                kerns.append((twice * twice) * (1.25 * LOG2E - taper) * jnp.exp2(taper))
            kern = jnp.concatenate(kerns, axis=1)
            high_part = kern.astype(jnp.bfloat16)
            low_part = (kern - high_part.astype(jnp.float32)).astype(jnp.bfloat16)
            both = jnp.concatenate([high_part, low_part], axis=0)
            result = jnp.dot(wts[chunk], both, preferred_element_type=jnp.float32)
            stage[m] += result[0:samples] + result[samples : 2 * samples]
            done = chunk + 1 >= high_of(m)
            after = jnp.minimum(m + 1, bands)
            chunk = jnp.where(done, low_of(after), chunk + 1)
            chunk = jnp.where(after == bands, jnp.where(done, 0, chunk), chunk)
            m = jnp.where(done, after, m)
        return m, chunk

    lax.fori_loop(0, (items + UNROLL - 1) // UNROLL, eval_items, (jnp.int32(0), low_of(jnp.int32(0))))

    part = lax.broadcasted_iota(jnp.int32, (samples, LANES), 1) // band

    def lay_out_pair(pair, carry):
        for half in range(2):
            lay_out(2 * pair + half)
        return carry

    def lay_out(block):
        at = pl.multiple_of(block * LANES, LANES)
        for group in range(groups):
            pieces = [
                stage[block * per_group + j, :, group * LANES : (group + 1) * LANES]
                for j in range(per_group)
            ]
            bit = 1
            while bit < per_group:
                keep = (part & bit) == 0
                for j in range(per_group):
                    if j & bit == 0:
                        first, second = pieces[j], pieces[j | bit]
                        pieces[j] = jnp.where(keep, first, pltpu.roll(second, bit * band, 1))
                        pieces[j | bit] = jnp.where(keep, pltpu.roll(first, LANES - bit * band, 1), second)
                bit *= 2
            for j in range(per_group):
                out_ref[group * per_group + j, :, pl.ds(at, LANES)] = pieces[j]

    lax.fori_loop(0, height // (2 * LANES), lay_out_pair, 0)


def pack_kernel(lat_hbm, lon_hbm, weights_hbm, count_ref, pack_ref, lat, sems, *, samples, slots):
    copies = [
        pltpu.make_async_copy(lat_hbm, lat, sems.at[0]),
        pltpu.make_async_copy(lon_hbm, pack_ref.at[samples + 1 : samples + 2], sems.at[1]),
        pltpu.make_async_copy(weights_hbm, pack_ref.at[0:samples], sems.at[2]),
    ]
    for copy in copies:
        copy.start()
    for copy in copies:
        copy.wait()
    slot = lax.broadcasted_iota(jnp.int32, (1, slots), 1)
    pack_ref[samples : samples + 1, :] = jnp.where(slot < count_ref[0], lat[...], FAR)


def turn_kernel(
    x_hbm, kappa_hbm, low_ref, high_ref, beta_ref, noise, kap, sem_x, sem_k, *, samples, width, height
):
    segments = height // LANES
    tall = height * samples // LANES
    copies = [pltpu.make_async_copy(x_hbm.at[:, c, :], noise.at[c], sem_x.at[c]) for c in range(width)]
    copies.append(pltpu.make_async_copy(kappa_hbm, kap, sem_k))
    for copy in copies:
        copy.start()
    copies[-1].wait()
    for column in range(width):
        half = (low_ref, high_ref)[column // PASSES]
        for i in range(segments):
            piece = kap[column : column + 1, i * LANES : (i + 1) * LANES]
            half[column % PASSES, tall + i : tall + i + 1, :] = piece
        beta_ref[column] = spread_kappa(half.at[column % PASSES], tall, samples, segments)
    for column in range(width):
        copies[column].wait()
    for column in range(width):
        half = (low_ref, high_ref)[column // PASSES]
        pieces = [noise[column, :, i * LANES : (i + 1) * LANES] for i in range(segments)]
        half[column % PASSES, 0:tall, :] = jnp.concatenate(pieces, axis=0).T


def spread_kappa(ref, start, samples, segments):
    rows = [ref[start + i : start + i + 1, :] - 0.5 for i in range(segments)]
    rows = [jnp.broadcast_to(row, (samples, LANES)) for row in rows]
    return jnp.concatenate(rows, axis=0).T


def prior_kernel(
    left_ref, low_ref, high_ref, right_ref, beta_ref, upd, out_hbm,
    noise, betas, first_y, second_y, result, sem_out, *, samples, width, height,
):
    halo = PASSES
    inner, outer = horner_coeffs()
    segments = height // LANES
    tall = height * samples // LANES
    columns = width + 2 * halo
    pitch = tall + 2 * PAD
    lane = lax.broadcasted_iota(jnp.int32, (8, LANES), 1)
    sub = lax.broadcasted_iota(jnp.int32, (8, LANES), 0)
    on_top, on_bottom = sub == 0, sub == 7
    inner_low = lane >= samples
    inner_high = lane < LANES - samples

    def at(base, offset):
        return pl.ds(pl.multiple_of(base + offset, 8), 8)

    def bring(column, carry):
        for k, ref in enumerate((left_ref, low_ref, high_ref, right_ref)):
            base = (k * halo + column) * pitch
            noise[pl.ds(pl.multiple_of(base + PAD, 8), tall), :] = ref[column, 0:tall, :]
        betas[column] = spread_kappa(left_ref.at[column], tall, samples, segments)
        betas[column + halo] = beta_ref[column]
        betas[column + 2 * halo] = beta_ref[column + halo]
        betas[column + 3 * halo] = spread_kappa(right_ref.at[column], tall, samples, segments)
        return carry

    lax.fori_loop(0, halo, bring, 0)
    source = noise
    for turn in range(PASSES):
        target = (first_y, second_y)[turn % 2]
        level = PASSES - 1 - turn
        last = turn == PASSES - 1

        def sweep(column, count, source=source, target=target, level=level, last=last):
            base = column * pitch
            saved = [[] for _ in range(count)]
            for r in range(tall // 8):
                row = PAD + r * 8
                line = [source[at(base, t * pitch + row), :] for t in range(-1, count + 1)]
                for t in range(count):
                    north = source[pl.ds(base + (t * pitch + row - 1), 8), :]
                    south = source[pl.ds(base + (t * pitch + row + 1), 8), :]
                    if r == 0:
                        end = source[pl.ds(base + (t * pitch + PAD + tall - 1), 8), :]
                        end = jnp.where(inner_low, pltpu.roll(end, samples, 1), 0.0)
                        north = jnp.where(on_top, end, north)
                    if r == tall // 8 - 1:
                        end = source[pl.ds(base + (t * pitch + PAD - 7), 8), :]
                        end = jnp.where(inner_high, pltpu.roll(end, LANES - samples, 1), 0.0)
                        south = jnp.where(on_bottom, end, south)
                    beside = (north + south) + (line[t] + line[t + 2])
                    value = beside - betas[column + t, r * 8 : r * 8 + 8, :] * line[t + 1]
                    value = value + inner[level] * noise[at(base, t * pitch + row), :]
                    if last:
                        saved[t].append(value)
                    else:
                        target[at(base, t * pitch + row), :] = value
            for t in range(count if last else 0):
                own = column + t - halo
                turned = jnp.concatenate(saved[t], axis=0).T
                for i in range(segments):
                    lanes = slice(i * LANES, (i + 1) * LANES)
                    value = outer * turned[i * samples : (i + 1) * samples, :] + upd[own, :, lanes]
                    result[own, :, lanes] = value
                pltpu.make_async_copy(result.at[own], out_hbm.at[:, own, :], sem_out.at[own]).start()

        def step_wide(step, carry, sweep=sweep, turn=turn):
            sweep(turn + 1 + WIDE * step, WIDE)
            return carry

        count = columns - 2 * (turn + 1)
        lax.fori_loop(0, count // WIDE, step_wide, 0)
        if count % WIDE:
            sweep(jnp.int32(turn + 1 + count - count % WIDE), count % WIDE)
        source = target
    for column in range(width):
        pltpu.make_async_copy(result.at[column], out_hbm.at[:, column, :], sem_out.at[column]).wait()


def shift_to(value, axis, steps):
    count = lax.axis_size(axis)
    return lax.ppermute(value, axis, [(source, (source + steps) % count) for source in range(count)])


def local(white_noise, kappa_sq, station_lat, station_lon, station_weights, station_count):
    samples, width, height = white_noise.shape
    slots = station_lat.shape[0]
    halo = PASSES
    anywhere = pl.BlockSpec(memory_space=pl.ANY)
    whole = pl.BlockSpec(memory_space=pltpu.VMEM)
    hbm = pl.BlockSpec(memory_space=pltpu.HBM)

    def in_hbm(items):
        return [pltpu.with_memory_space_constraint(item, pltpu.HBM) for item in items]

    pack = pl.pallas_call(
        lambda *refs: pack_kernel(*refs, samples=samples, slots=slots),
        out_shape=pltpu.VMEM((samples + 2, slots), jnp.float32),
        in_specs=[hbm] * 3 + [pl.BlockSpec(memory_space=pltpu.SMEM)],
        out_specs=whole,
        scratch_shapes=[pltpu.VMEM((1, slots), jnp.float32), pltpu.SemaphoreType.DMA((3,))],
        compiler_params=pltpu.CompilerParams(vmem_limit_bytes=ROOM),
        name="pack",
    )(*in_hbm((station_lat[None], station_lon[None], station_weights)), station_count)
    later = lax.optimization_barrier((pack, white_noise, kappa_sq))
    pack = later[0]
    packs = []
    for step in range(-HOPS, HOPS + 1):
        packs.append(pack if step == 0 else shift_to(pack, "lon", -step))

    segments = height // LANES
    tall = height * samples // LANES
    half = pltpu.VMEM((halo, tall + segments, LANES), jnp.float32)
    low, high, beta = pl.pallas_call(
        lambda *refs: turn_kernel(*refs, samples=samples, width=width, height=height),
        out_shape=(half, half, pltpu.VMEM((width, tall, LANES), jnp.float32)),
        in_specs=[hbm] * 2,
        out_specs=(whole, whole, whole),
        scratch_shapes=[
            pltpu.VMEM((width, samples, height), jnp.float32),
            pltpu.VMEM((width, height), jnp.float32),
            pltpu.SemaphoreType.DMA((width,)),
            pltpu.SemaphoreType.DMA,
        ],
        compiler_params=pltpu.CompilerParams(vmem_limit_bytes=ROOM),
        name="turn",
    )(*in_hbm(later[1:]))
    left = shift_to(high, "lon", 1)
    right = shift_to(low, "lon", -1)
    packs = [pltpu.with_memory_space_constraint(item, pltpu.VMEM) for item in packs]

    lists = 2 * HOPS + 1
    band = HOPS * width
    bands = height // band
    rows_m = (bands + 1 + 7) // 8 * 8
    room = lists * slots + 2 * LANES
    upd = pl.pallas_call(
        lambda *refs: station_kernel(*refs, samples=samples, width=width, height=height, slots=slots),
        out_shape=pltpu.VMEM((width, samples, height), jnp.float32),
        in_specs=[whole] * lists,
        out_specs=whole,
        scratch_shapes=[
            pltpu.VMEM((8, lists * rows_m), jnp.int32),
            pltpu.SMEM((8, lists * rows_m), jnp.int32),
            pltpu.VMEM((lists, LANES, slots), jnp.bfloat16),
            pltpu.VMEM((room, LANES), jnp.float32),
            pltpu.VMEM((room, LANES), jnp.float32),
            pltpu.VMEM((room // CH, 2 * samples, 2 * CH), jnp.bfloat16),
            pltpu.VMEM((room, LANES), jnp.float32),
            pltpu.VMEM((room, band * width), jnp.float32),
            pltpu.VMEM((bands + 1, samples, band * width), jnp.float32),
            pltpu.SMEM((bands + 1,), jnp.int32),
            pltpu.SemaphoreType.DMA,
        ],
        compiler_params=pltpu.CompilerParams(vmem_limit_bytes=ROOM),
        cost_estimate=pl.CostEstimate(flops=10000000000, transcendentals=10**7, bytes_accessed=2 * 10**6),
        name="stations",
    )(*packs)
    columns = width + 2 * halo
    field = pltpu.VMEM(((columns + 2) * (tall + 2 * PAD), LANES), jnp.float32)
    fields = [left, low, high, right, beta, upd]
    fields = [pltpu.with_memory_space_constraint(item, pltpu.VMEM) for item in fields]
    return pl.pallas_call(
        lambda *refs: prior_kernel(*refs, samples=samples, width=width, height=height),
        out_shape=jax.ShapeDtypeStruct((samples, width, height), jnp.float32),
        in_specs=[whole] * 6,
        out_specs=anywhere,
        scratch_shapes=[
            field,
            pltpu.VMEM((columns + 2, tall, LANES), jnp.float32),
            field,
            field,
            pltpu.VMEM((width, samples, height), jnp.float32),
            pltpu.SemaphoreType.DMA((width,)),
        ],
        compiler_params=pltpu.CompilerParams(vmem_limit_bytes=ROOM),
        name="prior",
    )(*fields)


def solution(mesh):
    in_specs = (
        P("groups", "lon", None),
        P("lon", None),
        P(("groups", "lon")),
        P(("groups", "lon")),
        P("groups", "lon"),
        P(("groups", "lon")),
    )
    out_specs = P("groups", "lon", None)
    return jax.shard_map(local, mesh=mesh, in_specs=in_specs, out_specs=out_specs, check_vma=False)
```

```python
import math

import jax
import jax.numpy as jnp
import numpy as np
from jax import lax
from jax.experimental import pallas as pl
from jax.experimental.pallas import tpu as pltpu
from jax.sharding import PartitionSpec as P

PASSES = 8
HOPS = 2
CHEB = (0.62, -0.41, 0.3, -0.22, 0.16, -0.115, 0.08, -0.055, 0.04)
LOG2E = math.log2(math.e)
FAR = 4096.0
CH = 32
UNROLL = 24
LANES = 128
BLOCK = 128
ROOM = 24 * 2**20
PAD = 8
WIDE = 8


def horner_coeffs():
    powers = np.polynomial.chebyshev.cheb2poly(np.array(CHEB))
    lead = powers[PASSES]
    inner = [float(powers[k] / lead * (-4.5) ** (PASSES - k)) for k in range(PASSES)]
    return inner, float(lead / 4.5**PASSES)


def split3(value):
    high = value.astype(jnp.bfloat16)
    rest = value - high.astype(jnp.float32)
    middle = rest.astype(jnp.bfloat16)
    low = (rest - middle.astype(jnp.float32)).astype(jnp.bfloat16)
    return high, middle, low


def station_kernel(
    p0, p1, p2, p3, p4, out_ref,
    table_v, table_s, data, sorted_s, merged, wts, latb, dlon2, stage, starts, sem_s,
    *, samples, width, height, slots,
):
    packs = (p0, p1, p2, p3, p4)
    lists = len(packs)
    radius = float(HOPS * width)
    band = int(radius)
    bands = height // band
    rows_m = (bands + 1 + 7) // 8 * 8
    scale = LOG2E / radius
    groups = band * width // LANES
    per_group = LANES // band
    index_m = lax.broadcasted_iota(jnp.int32, (rows_m, slots), 0).astype(jnp.float32)
    equal, below, onehot = [], [], []
    for pack in packs:
        lat = pack[samples : samples + 1, :]
        bucket = jnp.minimum(jnp.floor(lat * (1.0 / radius)), float(bands - 1))
        bucket = jnp.where(lat > FAR * 0.5, float(bands), bucket)
        bucket = jnp.broadcast_to(bucket, (rows_m, slots))
        equal.append(jnp.where(bucket == index_m, 1.0, 0.0))
        below.append(jnp.where(bucket < index_m, 1.0, 0.0).astype(jnp.bfloat16))
    before = lax.broadcasted_iota(jnp.int32, (slots, slots), 0) < lax.broadcasted_iota(
        jnp.int32, (slots, slots), 1
    )
    before = jnp.where(before, 1.0, 0.0).astype(jnp.bfloat16)
    all_below = jnp.concatenate(below, axis=0)
    inside = jnp.dot(
        jnp.concatenate(equal, axis=0).astype(jnp.bfloat16), before, preferred_element_type=jnp.float32
    )
    base = jnp.dot(all_below, jnp.ones((slots, LANES), jnp.bfloat16), preferred_element_type=jnp.float32)
    counts = lax.dot_general(
        jnp.ones((8, slots), jnp.bfloat16), all_below, (((1,), (1,)), ((), ())),
        preferred_element_type=jnp.float32,
    )
    table_v[...] = counts.astype(jnp.int32)
    copy = pltpu.make_async_copy(table_v, table_s, sem_s)
    copy.start()
    ranks = []
    for index in range(lists):
        rows = slice(index * rows_m, (index + 1) * rows_m)
        start = base[rows]
        start = jnp.concatenate([start] * (slots // LANES), axis=1)
        ranks.append(jnp.sum(equal[index] * (inside[rows] + start), axis=0, keepdims=True))

    factor = 4.0 * math.exp(-1.0) / LOG2E**5
    for index, pack in enumerate(packs):
        weights = pack[0:samples, :] * factor
        w_high = weights.astype(jnp.bfloat16)
        w_low = (weights - w_high.astype(jnp.float32)).astype(jnp.bfloat16)
        lat = pack[samples : samples + 1, :]
        lon = pack[samples + 1 : samples + 2, :] + float((index - HOPS) * width)
        parts = split3(lat) + split3(lon)
        parts = [part.astype(jnp.float32) for part in parts]
        filler = jnp.zeros((LANES - 2 * samples - 6, slots), jnp.float32)
        block = jnp.concatenate(
            [w_high.astype(jnp.float32), w_low.astype(jnp.float32)] + parts + [filler], axis=0
        )
        data[index] = block.astype(jnp.bfloat16)

    copy.wait()

    row_p = lax.broadcasted_iota(jnp.int32, (LANES, slots), 0).astype(jnp.float32)
    longest = table_s[0, bands]
    for index in range(1, lists):
        longest = jnp.maximum(longest, table_s[0, index * rows_m + bands])

    def sort_block(block, carry):
        first = block * LANES
        for index in range(lists):
            pick = ranks[index] - first.astype(jnp.float32)
            pick = jnp.where(jnp.broadcast_to(pick, (LANES, slots)) == row_p, 1.0, 0.0)
            moved = lax.dot_general(
                pick.astype(jnp.bfloat16), data[index], (((1,), (1,)), ((), ())),
                preferred_element_type=jnp.float32,
            )
            sorted_s[pl.ds(pl.multiple_of(index * slots + first, LANES), LANES), :] = moved
        return carry

    lax.fori_loop(0, (longest + LANES - 1) // LANES, sort_block, 0)

    step = 32

    def merge_band(m, position):
        starts[m] = position
        begins, sizes, places = [], [], []
        for index in range(lists):
            begin = table_s[0, index * rows_m + m]
            sizes.append(table_s[0, index * rows_m + m + 1] - begin)
            begins.append(index * slots + begin)
            places.append(position)
            position = position + sizes[-1]
        for index in range(lists):
            merged[pl.ds(places[index], step), :] = sorted_s[pl.ds(begins[index], step), :]
        largest = sizes[0]
        for size in sizes[1:]:
            largest = jnp.maximum(largest, size)

        @pl.when(largest > step)
        def _():
            for index in range(lists):

                def more(k, carry, index=index):
                    rows = sorted_s[pl.ds(begins[index] + k * step, step), :]
                    merged[pl.ds(places[index] + k * step, step), :] = rows
                    return carry

                lax.fori_loop(0, (sizes[index] + step - 1) // step, more, 0)

        return position

    total = lax.fori_loop(0, bands, merge_band, jnp.int32(0))
    starts[bands] = total
    lane = lax.broadcasted_iota(jnp.int32, (BLOCK, LANES), 1)
    merged[pl.ds(total, BLOCK), :] = jnp.where(lane == 2 * samples, FAR, 0.0)

    lane_row = lax.broadcasted_iota(jnp.int32, (1, LANES), 1)
    cell_in = (lane_row % band).astype(jnp.float32)
    cell_lon = (lane_row // band).astype(jnp.float32)

    row_of = lax.broadcasted_iota(jnp.int32, (LANES, 2 * LANES), 0) - 2 * samples
    part_of = lax.broadcasted_iota(jnp.int32, (LANES, 2 * LANES), 1) // LANES * 3
    gather = jnp.where((row_of >= part_of) & (row_of < part_of + 3), 1.0, 0.0).astype(jnp.bfloat16)
    turn_rows = lax.broadcasted_iota(jnp.int32, (samples, LANES), 0)
    turn_lanes = lax.broadcasted_iota(jnp.int32, (samples, LANES), 1)
    select = (turn_lanes == turn_rows) | (turn_lanes == turn_rows + samples)
    select = jnp.where(select, 1.0, 0.0).astype(jnp.bfloat16)
    is_high = lax.broadcasted_iota(jnp.int32, (CH, LANES), 1) < samples

    def prepare_pair(pair, carry):
        for half in range(2):
            prepare(2 * pair + half)
        return carry

    def prepare(block):
        first = pl.multiple_of(block * BLOCK, BLOCK)
        rows = merged[pl.ds(first, BLOCK), :]
        places = jnp.dot(rows.astype(jnp.bfloat16), gather, preferred_element_type=jnp.float32)
        latb[pl.ds(first, BLOCK), :] = places[:, 0:LANES]
        lon = places[:, LANES : 2 * LANES]
        for group in range(groups):
            offset = (lon - (cell_lon + float(group * per_group))) * scale
            dlon2[pl.ds(first, BLOCK), group * LANES : (group + 1) * LANES] = offset * offset + 1e-30
        for k in range(BLOCK // CH):
            some = rows[k * CH : (k + 1) * CH, :]
            high_rows = jnp.where(is_high, some, 0.0)
            low_rows = jnp.where(is_high, 0.0, some)
            thrice = jnp.concatenate([high_rows, high_rows, low_rows], axis=0).astype(jnp.bfloat16)
            turned = lax.dot_general(
                select, thrice, (((1,), (1,)), ((), ())), preferred_element_type=jnp.float32
            )
            wts[block * (BLOCK // CH) + k] = turned.astype(jnp.bfloat16)

    lax.fori_loop(0, total // (2 * BLOCK) + 1, prepare_pair, 0)

    def low_of(m):
        return starts[jnp.maximum(m - 1, 0)] // CH

    def high_of(m):
        return jnp.maximum((starts[jnp.minimum(m + 2, bands)] + CH - 1) // CH, low_of(m) + 1)

    items = lax.fori_loop(0, bands, lambda m, count: count + high_of(m) - low_of(m), jnp.int32(0))
    for m in range(bands + 1):
        stage[m] = jnp.zeros((samples, groups * LANES), jnp.float32)

    def eval_items(step, carry):
        m, chunk = carry
        for _ in range(UNROLL):
            first = pl.multiple_of(chunk * CH, CH)
            offset = (latb[pl.ds(first, CH), :] - (cell_in + (m * band).astype(jnp.float32))) * scale
            offset = offset * offset
            kerns = []
            for group in range(groups):
                square = offset + dlon2[pl.ds(first, CH), group * LANES : (group + 1) * LANES]
                taper = jnp.maximum(LOG2E - square * lax.rsqrt(square), 0.0)
                twice = taper * taper
                kerns.append((twice * twice) * (1.25 * LOG2E - taper) * jnp.exp2(taper))
            kern = jnp.concatenate(kerns, axis=1)
            high_part = kern.astype(jnp.bfloat16)
            low_part = (kern - high_part.astype(jnp.float32)).astype(jnp.bfloat16)
            parts = jnp.concatenate([high_part, low_part, high_part], axis=0)
            stage[m] += jnp.dot(wts[chunk], parts, preferred_element_type=jnp.float32)
            done = chunk + 1 >= high_of(m)
            after = jnp.minimum(m + 1, bands)
            chunk = jnp.where(done, low_of(after), chunk + 1)
            chunk = jnp.where(after == bands, jnp.where(done, 0, chunk), chunk)
            m = jnp.where(done, after, m)
        return m, chunk

    lax.fori_loop(0, (items + UNROLL - 1) // UNROLL, eval_items, (jnp.int32(0), low_of(jnp.int32(0))))

    part = lax.broadcasted_iota(jnp.int32, (samples, LANES), 1) // band

    def lay_out_pair(pair, carry):
        for half in range(2):
            lay_out(2 * pair + half)
        return carry

    def lay_out(block):
        at = pl.multiple_of(block * LANES, LANES)
        for group in range(groups):
            pieces = [
                stage[block * per_group + j, :, group * LANES : (group + 1) * LANES]
                for j in range(per_group)
            ]
            bit = 1
            while bit < per_group:
                keep = (part & bit) == 0
                for j in range(per_group):
                    if j & bit == 0:
                        first, second = pieces[j], pieces[j | bit]
                        pieces[j] = jnp.where(keep, first, pltpu.roll(second, bit * band, 1))
                        pieces[j | bit] = jnp.where(keep, pltpu.roll(first, LANES - bit * band, 1), second)
                bit *= 2
            for j in range(per_group):
                out_ref[group * per_group + j, :, pl.ds(at, LANES)] = pieces[j]

    lax.fori_loop(0, height // (2 * LANES), lay_out_pair, 0)


def pack_kernel(lat_hbm, lon_hbm, weights_hbm, count_ref, pack_ref, lat, sems, *, samples, slots):
    copies = [
        pltpu.make_async_copy(lat_hbm, lat, sems.at[0]),
        pltpu.make_async_copy(lon_hbm, pack_ref.at[samples + 1 : samples + 2], sems.at[1]),
        pltpu.make_async_copy(weights_hbm, pack_ref.at[0:samples], sems.at[2]),
    ]
    for copy in copies:
        copy.start()
    for copy in copies:
        copy.wait()
    slot = lax.broadcasted_iota(jnp.int32, (1, slots), 1)
    pack_ref[samples : samples + 1, :] = jnp.where(slot < count_ref[0], lat[...], FAR)


def turn_kernel(
    x_hbm, kappa_hbm, low_ref, high_ref, beta_ref, noise, kap, sem_x, sem_k, *, samples, width, height
):
    segments = height // LANES
    tall = height * samples // LANES
    copies = [pltpu.make_async_copy(x_hbm.at[:, c, :], noise.at[c], sem_x.at[c]) for c in range(width)]
    copies.append(pltpu.make_async_copy(kappa_hbm, kap, sem_k))
    for copy in copies:
        copy.start()
    copies[-1].wait()
    for column in range(width):
        half = (low_ref, high_ref)[column // PASSES]
        for i in range(segments):
            piece = kap[column : column + 1, i * LANES : (i + 1) * LANES]
            half[column % PASSES, tall + i : tall + i + 1, :] = piece
        beta_ref[column] = spread_kappa(half.at[column % PASSES], tall, samples, segments)
    for column in range(width):
        copies[column].wait()
    for column in range(width):
        half = (low_ref, high_ref)[column // PASSES]
        pieces = [noise[column, :, i * LANES : (i + 1) * LANES] for i in range(segments)]
        half[column % PASSES, 0:tall, :] = jnp.concatenate(pieces, axis=0).T


def spread_kappa(ref, start, samples, segments):
    rows = [ref[start + i : start + i + 1, :] - 0.5 for i in range(segments)]
    rows = [jnp.broadcast_to(row, (samples, LANES)) for row in rows]
    return jnp.concatenate(rows, axis=0).T


def prior_kernel(
    left_ref, low_ref, high_ref, right_ref, beta_ref, upd, out_hbm,
    noise, betas, first_y, second_y, result, sem_out, *, samples, width, height,
):
    halo = PASSES
    inner, outer = horner_coeffs()
    segments = height // LANES
    tall = height * samples // LANES
    columns = width + 2 * halo
    pitch = tall + 2 * PAD
    lane = lax.broadcasted_iota(jnp.int32, (8, LANES), 1)
    sub = lax.broadcasted_iota(jnp.int32, (8, LANES), 0)
    on_top, on_bottom = sub == 0, sub == 7
    inner_low = lane >= samples
    inner_high = lane < LANES - samples

    def at(base, offset):
        return pl.ds(pl.multiple_of(base + offset, 8), 8)

    def bring(column, carry):
        for k, ref in enumerate((left_ref, low_ref, high_ref, right_ref)):
            base = (k * halo + column) * pitch
            noise[pl.ds(pl.multiple_of(base + PAD, 8), tall), :] = ref[column, 0:tall, :]
        betas[column] = spread_kappa(left_ref.at[column], tall, samples, segments)
        betas[column + halo] = beta_ref[column]
        betas[column + 2 * halo] = beta_ref[column + halo]
        betas[column + 3 * halo] = spread_kappa(right_ref.at[column], tall, samples, segments)
        return carry

    lax.fori_loop(0, halo, bring, 0)
    source = noise
    for turn in range(PASSES):
        target = (first_y, second_y)[turn % 2]
        level = PASSES - 1 - turn
        last = turn == PASSES - 1

        def sweep(column, count, source=source, target=target, level=level, last=last):
            base = column * pitch
            saved = [[] for _ in range(count)]
            for r in range(tall // 8):
                row = PAD + r * 8
                line = [source[at(base, t * pitch + row), :] for t in range(-1, count + 1)]
                for t in range(count):
                    north = source[pl.ds(base + (t * pitch + row - 1), 8), :]
                    south = source[pl.ds(base + (t * pitch + row + 1), 8), :]
                    if r == 0:
                        end = source[pl.ds(base + (t * pitch + PAD + tall - 1), 8), :]
                        end = jnp.where(inner_low, pltpu.roll(end, samples, 1), 0.0)
                        north = jnp.where(on_top, end, north)
                    if r == tall // 8 - 1:
                        end = source[pl.ds(base + (t * pitch + PAD - 7), 8), :]
                        end = jnp.where(inner_high, pltpu.roll(end, LANES - samples, 1), 0.0)
                        south = jnp.where(on_bottom, end, south)
                    beside = (north + south) + (line[t] + line[t + 2])
                    value = beside - betas[column + t, r * 8 : r * 8 + 8, :] * line[t + 1]
                    value = value + inner[level] * noise[at(base, t * pitch + row), :]
                    if last:
                        saved[t].append(value)
                    else:
                        target[at(base, t * pitch + row), :] = value
            for t in range(count if last else 0):
                own = column + t - halo
                turned = jnp.concatenate(saved[t], axis=0).T
                for i in range(segments):
                    lanes = slice(i * LANES, (i + 1) * LANES)
                    value = outer * turned[i * samples : (i + 1) * samples, :] + upd[own, :, lanes]
                    result[own, :, lanes] = value
                pltpu.make_async_copy(result.at[own], out_hbm.at[:, own, :], sem_out.at[own]).start()

        def step_wide(step, carry, sweep=sweep, turn=turn):
            sweep(turn + 1 + WIDE * step, WIDE)
            return carry

        count = columns - 2 * (turn + 1)
        lax.fori_loop(0, count // WIDE, step_wide, 0)
        if count % WIDE:
            sweep(jnp.int32(turn + 1 + count - count % WIDE), count % WIDE)
        source = target
    for column in range(width):
        pltpu.make_async_copy(result.at[column], out_hbm.at[:, column, :], sem_out.at[column]).wait()


def shift_to(value, axis, steps):
    count = lax.axis_size(axis)
    return lax.ppermute(value, axis, [(source, (source + steps) % count) for source in range(count)])


def local(white_noise, kappa_sq, station_lat, station_lon, station_weights, station_count):
    samples, width, height = white_noise.shape
    slots = station_lat.shape[0]
    halo = PASSES
    anywhere = pl.BlockSpec(memory_space=pl.ANY)
    whole = pl.BlockSpec(memory_space=pltpu.VMEM)
    hbm = pl.BlockSpec(memory_space=pltpu.HBM)

    def in_hbm(items):
        return [pltpu.with_memory_space_constraint(item, pltpu.HBM) for item in items]

    pack = pl.pallas_call(
        lambda *refs: pack_kernel(*refs, samples=samples, slots=slots),
        out_shape=pltpu.VMEM((samples + 2, slots), jnp.float32),
        in_specs=[hbm] * 3 + [pl.BlockSpec(memory_space=pltpu.SMEM)],
        out_specs=whole,
        scratch_shapes=[pltpu.VMEM((1, slots), jnp.float32), pltpu.SemaphoreType.DMA((3,))],
        compiler_params=pltpu.CompilerParams(vmem_limit_bytes=ROOM),
        name="pack",
    )(*in_hbm((station_lat[None], station_lon[None], station_weights)), station_count)
    later = lax.optimization_barrier((pack, white_noise, kappa_sq))
    pack = later[0]
    packs = []
    for step in range(-HOPS, HOPS + 1):
        packs.append(pack if step == 0 else shift_to(pack, "lon", -step))

    segments = height // LANES
    tall = height * samples // LANES
    half = pltpu.VMEM((halo, tall + segments, LANES), jnp.float32)
    low, high, beta = pl.pallas_call(
        lambda *refs: turn_kernel(*refs, samples=samples, width=width, height=height),
        out_shape=(half, half, pltpu.VMEM((width, tall, LANES), jnp.float32)),
        in_specs=[hbm] * 2,
        out_specs=(whole, whole, whole),
        scratch_shapes=[
            pltpu.VMEM((width, samples, height), jnp.float32),
            pltpu.VMEM((width, height), jnp.float32),
            pltpu.SemaphoreType.DMA((width,)),
            pltpu.SemaphoreType.DMA,
        ],
        compiler_params=pltpu.CompilerParams(vmem_limit_bytes=ROOM),
        name="turn",
    )(*in_hbm(later[1:]))
    left = shift_to(high, "lon", 1)
    right = shift_to(low, "lon", -1)
    packs = [pltpu.with_memory_space_constraint(item, pltpu.VMEM) for item in packs]

    lists = 2 * HOPS + 1
    band = HOPS * width
    bands = height // band
    rows_m = (bands + 1 + 7) // 8 * 8
    room = lists * slots + 2 * LANES
    upd = pl.pallas_call(
        lambda *refs: station_kernel(*refs, samples=samples, width=width, height=height, slots=slots),
        out_shape=pltpu.VMEM((width, samples, height), jnp.float32),
        in_specs=[whole] * lists,
        out_specs=whole,
        scratch_shapes=[
            pltpu.VMEM((8, lists * rows_m), jnp.int32),
            pltpu.SMEM((8, lists * rows_m), jnp.int32),
            pltpu.VMEM((lists, LANES, slots), jnp.bfloat16),
            pltpu.VMEM((room, LANES), jnp.float32),
            pltpu.VMEM((room, LANES), jnp.float32),
            pltpu.VMEM((room // CH, samples, 3 * CH), jnp.bfloat16),
            pltpu.VMEM((room, LANES), jnp.float32),
            pltpu.VMEM((room, band * width), jnp.float32),
            pltpu.VMEM((bands + 1, samples, band * width), jnp.float32),
            pltpu.SMEM((bands + 1,), jnp.int32),
            pltpu.SemaphoreType.DMA,
        ],
        compiler_params=pltpu.CompilerParams(vmem_limit_bytes=ROOM),
        cost_estimate=pl.CostEstimate(flops=10000000000, transcendentals=10**7, bytes_accessed=2 * 10**6),
        name="stations",
    )(*packs)
    columns = width + 2 * halo
    field = pltpu.VMEM(((columns + 2) * (tall + 2 * PAD), LANES), jnp.float32)
    fields = [left, low, high, right, beta, upd]
    fields = [pltpu.with_memory_space_constraint(item, pltpu.VMEM) for item in fields]
    return pl.pallas_call(
        lambda *refs: prior_kernel(*refs, samples=samples, width=width, height=height),
        out_shape=jax.ShapeDtypeStruct((samples, width, height), jnp.float32),
        in_specs=[whole] * 6,
        out_specs=anywhere,
        scratch_shapes=[
            field,
            pltpu.VMEM((columns + 2, tall, LANES), jnp.float32),
            field,
            field,
            pltpu.VMEM((width, samples, height), jnp.float32),
            pltpu.SemaphoreType.DMA((width,)),
        ],
        compiler_params=pltpu.CompilerParams(vmem_limit_bytes=ROOM),
        name="prior",
    )(*fields)


def solution(mesh):
    in_specs = (
        P("groups", "lon", None),
        P("lon", None),
        P(("groups", "lon")),
        P(("groups", "lon")),
        P("groups", "lon"),
        P(("groups", "lon")),
    )
    out_specs = P("groups", "lon", None)
    return jax.shard_map(local, mesh=mesh, in_specs=in_specs, out_specs=out_specs, check_vma=False)
```

```python
import math

import jax
import jax.numpy as jnp
import numpy as np
from jax import lax
from jax.experimental import pallas as pl
from jax.experimental.pallas import tpu as pltpu
from jax.sharding import PartitionSpec as P

PASSES = 8
HOPS = 2
CHEB = (0.62, -0.41, 0.3, -0.22, 0.16, -0.115, 0.08, -0.055, 0.04)
LOG2E = math.log2(math.e)
FAR = 4096.0
CH = 32
UNROLL = 24
LANES = 128
BLOCK = 128
ROOM = 24 * 2**20
PAD = 8
WIDE = 8


def horner_coeffs():
    powers = np.polynomial.chebyshev.cheb2poly(np.array(CHEB))
    lead = powers[PASSES]
    inner = [float(powers[k] / lead * (-4.5) ** (PASSES - k)) for k in range(PASSES)]
    return inner, float(lead / 4.5**PASSES)


def split3(value):
    high = value.astype(jnp.bfloat16)
    rest = value - high.astype(jnp.float32)
    middle = rest.astype(jnp.bfloat16)
    low = (rest - middle.astype(jnp.float32)).astype(jnp.bfloat16)
    return high, middle, low


def station_kernel(
    p0, p1, p2, p3, p4, out_ref,
    table_v, table_s, data, sorted_s, merged, wts, latb, dlon2, stage, starts, sem_s,
    *, samples, width, height, slots,
):
    packs = (p0, p1, p2, p3, p4)
    lists = len(packs)
    radius = float(HOPS * width)
    band = int(radius)
    bands = height // band
    rows_m = (bands + 1 + 7) // 8 * 8
    scale = LOG2E / radius
    groups = band * width // LANES
    per_group = LANES // band
    index_m = lax.broadcasted_iota(jnp.int32, (rows_m, slots), 0).astype(jnp.float32)
    equal, below, onehot = [], [], []
    for pack in packs:
        lat = pack[samples : samples + 1, :]
        bucket = jnp.minimum(jnp.floor(lat * (1.0 / radius)), float(bands - 1))
        bucket = jnp.where(lat > FAR * 0.5, float(bands), bucket)
        bucket = jnp.broadcast_to(bucket, (rows_m, slots))
        equal.append(jnp.where(bucket == index_m, 1.0, 0.0))
        below.append(jnp.where(bucket < index_m, 1.0, 0.0).astype(jnp.bfloat16))
    before = lax.broadcasted_iota(jnp.int32, (slots, slots), 0) < lax.broadcasted_iota(
        jnp.int32, (slots, slots), 1
    )
    before = jnp.where(before, 1.0, 0.0).astype(jnp.bfloat16)
    all_below = jnp.concatenate(below, axis=0)
    inside = jnp.dot(
        jnp.concatenate(equal, axis=0).astype(jnp.bfloat16), before, preferred_element_type=jnp.float32
    )
    base = jnp.dot(all_below, jnp.ones((slots, LANES), jnp.bfloat16), preferred_element_type=jnp.float32)
    counts = lax.dot_general(
        jnp.ones((8, slots), jnp.bfloat16), all_below, (((1,), (1,)), ((), ())),
        preferred_element_type=jnp.float32,
    )
    table_v[...] = counts.astype(jnp.int32)
    copy = pltpu.make_async_copy(table_v, table_s, sem_s)
    copy.start()
    ranks = []
    for index in range(lists):
        rows = slice(index * rows_m, (index + 1) * rows_m)
        start = base[rows]
        start = jnp.concatenate([start] * (slots // LANES), axis=1)
        ranks.append(jnp.sum(equal[index] * (inside[rows] + start), axis=0, keepdims=True))

    factor = 4.0 * math.exp(-1.0) / LOG2E**5
    for index, pack in enumerate(packs):
        weights = pack[0:samples, :] * factor
        w_high = weights.astype(jnp.bfloat16)
        w_low = (weights - w_high.astype(jnp.float32)).astype(jnp.bfloat16)
        lat = pack[samples : samples + 1, :]
        lon = pack[samples + 1 : samples + 2, :] + float((index - HOPS) * width)
        parts = split3(lat) + split3(lon)
        parts = [part.astype(jnp.float32) for part in parts]
        filler = jnp.zeros((LANES - 2 * samples - 6, slots), jnp.float32)
        block = jnp.concatenate(
            [w_high.astype(jnp.float32), w_low.astype(jnp.float32)] + parts + [filler], axis=0
        )
        data[index] = block.astype(jnp.bfloat16)

    for m in range(bands + 1):
        stage[m] = jnp.zeros((samples, groups * LANES), jnp.float32)
    copy.wait()

    row_p = lax.broadcasted_iota(jnp.int32, (LANES, slots), 0).astype(jnp.float32)
    longest = table_s[0, bands]
    for index in range(1, lists):
        longest = jnp.maximum(longest, table_s[0, index * rows_m + bands])

    def sort_block(block, carry):
        first = block * LANES
        for index in range(lists):
            pick = ranks[index] - first.astype(jnp.float32)
            pick = jnp.where(jnp.broadcast_to(pick, (LANES, slots)) == row_p, 1.0, 0.0)
            moved = lax.dot_general(
                pick.astype(jnp.bfloat16), data[index], (((1,), (1,)), ((), ())),
                preferred_element_type=jnp.float32,
            )
            sorted_s[pl.ds(pl.multiple_of(index * slots + first, LANES), LANES), :] = moved
        return carry

    def sort_pair(pair, carry):
        return sort_block(2 * pair + 1, sort_block(2 * pair, carry))

    lax.fori_loop(0, (longest + 2 * LANES - 1) // (2 * LANES), sort_pair, 0)

    step = 32

    def merge_band(m, position):
        starts[m] = position
        begins, sizes, places = [], [], []
        for index in range(lists):
            begin = table_s[0, index * rows_m + m]
            sizes.append(table_s[0, index * rows_m + m + 1] - begin)
            begins.append(index * slots + begin)
            places.append(position)
            position = position + sizes[-1]
        for index in range(lists):
            merged[pl.ds(places[index], step), :] = sorted_s[pl.ds(begins[index], step), :]
        largest = sizes[0]
        for size in sizes[1:]:
            largest = jnp.maximum(largest, size)

        @pl.when(largest > step)
        def _():
            for index in range(lists):

                def more(k, carry, index=index):
                    rows = sorted_s[pl.ds(begins[index] + k * step, step), :]
                    merged[pl.ds(places[index] + k * step, step), :] = rows
                    return carry

                lax.fori_loop(0, (sizes[index] + step - 1) // step, more, 0)

        return position

    def merge_pair(pair, position):
        return merge_band(2 * pair + 1, merge_band(2 * pair, position))

    total = lax.fori_loop(0, bands // 2, merge_pair, jnp.int32(0))
    starts[bands] = total
    lane = lax.broadcasted_iota(jnp.int32, (BLOCK, LANES), 1)
    merged[pl.ds(total, BLOCK), :] = jnp.where(lane == 2 * samples, FAR, 0.0)

    lane_row = lax.broadcasted_iota(jnp.int32, (1, LANES), 1)
    cell_in = (lane_row % band).astype(jnp.float32)
    cell_lon = (lane_row // band).astype(jnp.float32)

    row_of = lax.broadcasted_iota(jnp.int32, (LANES, 2 * LANES), 0) - 2 * samples
    part_of = lax.broadcasted_iota(jnp.int32, (LANES, 2 * LANES), 1) // LANES * 3
    gather = jnp.where((row_of >= part_of) & (row_of < part_of + 3), 1.0, 0.0).astype(jnp.bfloat16)
    turn_rows = lax.broadcasted_iota(jnp.int32, (samples, LANES), 0)
    turn_lanes = lax.broadcasted_iota(jnp.int32, (samples, LANES), 1)
    select = (turn_lanes == turn_rows) | (turn_lanes == turn_rows + samples)
    select = jnp.where(select, 1.0, 0.0).astype(jnp.bfloat16)
    is_high = lax.broadcasted_iota(jnp.int32, (CH, LANES), 1) < samples

    def prepare_pair(pair, carry):
        for half in range(2):
            prepare(2 * pair + half)
        return carry

    def prepare(block):
        first = pl.multiple_of(block * BLOCK, BLOCK)
        rows = merged[pl.ds(first, BLOCK), :]
        places = jnp.dot(rows.astype(jnp.bfloat16), gather, preferred_element_type=jnp.float32)
        latb[pl.ds(first, BLOCK), :] = places[:, 0:LANES]
        lon = places[:, LANES : 2 * LANES]
        for group in range(groups):
            offset = (lon - (cell_lon + float(group * per_group))) * scale
            dlon2[pl.ds(first, BLOCK), group * LANES : (group + 1) * LANES] = offset * offset + 1e-30
        for k in range(BLOCK // CH):
            some = rows[k * CH : (k + 1) * CH, :]
            high_rows = jnp.where(is_high, some, 0.0)
            low_rows = jnp.where(is_high, 0.0, some)
            thrice = jnp.concatenate([high_rows, high_rows, low_rows], axis=0).astype(jnp.bfloat16)
            turned = lax.dot_general(
                select, thrice, (((1,), (1,)), ((), ())), preferred_element_type=jnp.float32
            )
            wts[block * (BLOCK // CH) + k] = turned.astype(jnp.bfloat16)

    lax.fori_loop(0, total // (2 * BLOCK) + 1, prepare_pair, 0)

    def low_of(m):
        return starts[jnp.maximum(m - 1, 0)] // CH

    def high_of(m):
        return jnp.maximum((starts[jnp.minimum(m + 2, bands)] + CH - 1) // CH, low_of(m) + 1)

    def eval_items(carry):
        m, chunk = carry
        for _ in range(UNROLL):
            first = pl.multiple_of(chunk * CH, CH)
            offset = (latb[pl.ds(first, CH), :] - (cell_in + (m * band).astype(jnp.float32))) * scale
            offset = offset * offset
            kerns = []
            for group in range(groups):
                square = offset + dlon2[pl.ds(first, CH), group * LANES : (group + 1) * LANES]
                taper = jnp.maximum(LOG2E - square * lax.rsqrt(square), 0.0)
                twice = taper * taper
                kerns.append((twice * twice) * (1.25 * LOG2E - taper) * jnp.exp2(taper))
            kern = jnp.concatenate(kerns, axis=1)
            high_part = kern.astype(jnp.bfloat16)
            low_part = (kern - high_part.astype(jnp.float32)).astype(jnp.bfloat16)
            parts = jnp.concatenate([high_part, low_part, high_part], axis=0)
            stage[m] += jnp.dot(wts[chunk], parts, preferred_element_type=jnp.float32)
            done = chunk + 1 >= high_of(m)
            after = jnp.minimum(m + 1, bands)
            chunk = jnp.where(done, low_of(after), chunk + 1)
            chunk = jnp.where(after == bands, jnp.where(done, 0, chunk), chunk)
            m = jnp.where(done, after, m)
        return m, chunk

    first_item = (jnp.int32(0), low_of(jnp.int32(0)))
    lax.while_loop(lambda carry: carry[0] < bands, eval_items, first_item)

    part = lax.broadcasted_iota(jnp.int32, (samples, LANES), 1) // band

    def lay_out_pair(pair, carry):
        for half in range(2):
            lay_out(2 * pair + half)
        return carry

    def lay_out(block):
        at = pl.multiple_of(block * LANES, LANES)
        for group in range(groups):
            pieces = [
                stage[block * per_group + j, :, group * LANES : (group + 1) * LANES]
                for j in range(per_group)
            ]
            bit = 1
            while bit < per_group:
                keep = (part & bit) == 0
                for j in range(per_group):
                    if j & bit == 0:
                        first, second = pieces[j], pieces[j | bit]
                        pieces[j] = jnp.where(keep, first, pltpu.roll(second, bit * band, 1))
                        pieces[j | bit] = jnp.where(keep, pltpu.roll(first, LANES - bit * band, 1), second)
                bit *= 2
            for j in range(per_group):
                out_ref[group * per_group + j, :, pl.ds(at, LANES)] = pieces[j]

    lax.fori_loop(0, height // (2 * LANES), lay_out_pair, 0)


def pack_kernel(lat_hbm, lon_hbm, weights_hbm, count_ref, pack_ref, lat, sems, *, samples, slots):
    copies = [
        pltpu.make_async_copy(lat_hbm, lat, sems.at[0]),
        pltpu.make_async_copy(lon_hbm, pack_ref.at[samples + 1 : samples + 2], sems.at[1]),
        pltpu.make_async_copy(weights_hbm, pack_ref.at[0:samples], sems.at[2]),
    ]
    for copy in copies:
        copy.start()
    for copy in copies:
        copy.wait()
    slot = lax.broadcasted_iota(jnp.int32, (1, slots), 1)
    pack_ref[samples : samples + 1, :] = jnp.where(slot < count_ref[0], lat[...], FAR)


def turn_kernel(
    x_hbm, kappa_hbm, low_ref, high_ref, beta_ref, noise, kap, sem_x, sem_k, *, samples, width, height
):
    segments = height // LANES
    tall = height * samples // LANES
    copies = [pltpu.make_async_copy(x_hbm.at[:, c, :], noise.at[c], sem_x.at[c]) for c in range(width)]
    copies.append(pltpu.make_async_copy(kappa_hbm, kap, sem_k))
    for copy in copies:
        copy.start()
    copies[-1].wait()
    for column in range(width):
        half = (low_ref, high_ref)[column // PASSES]
        for i in range(segments):
            piece = kap[column : column + 1, i * LANES : (i + 1) * LANES]
            half[column % PASSES, tall + i : tall + i + 1, :] = piece
        beta_ref[column] = spread_kappa(half.at[column % PASSES], tall, samples, segments)
    for column in range(width):
        copies[column].wait()
    for column in range(width):
        half = (low_ref, high_ref)[column // PASSES]
        pieces = [noise[column, :, i * LANES : (i + 1) * LANES] for i in range(segments)]
        half[column % PASSES, 0:tall, :] = jnp.concatenate(pieces, axis=0).T


def spread_kappa(ref, start, samples, segments):
    rows = [ref[start + i : start + i + 1, :] - 0.5 for i in range(segments)]
    rows = [jnp.broadcast_to(row, (samples, LANES)) for row in rows]
    return jnp.concatenate(rows, axis=0).T


def prior_kernel(
    left_ref, low_ref, high_ref, right_ref, beta_ref, upd, out_hbm,
    noise, betas, first_y, second_y, result, sem_out, *, samples, width, height,
):
    halo = PASSES
    inner, outer = horner_coeffs()
    segments = height // LANES
    tall = height * samples // LANES
    columns = width + 2 * halo
    pitch = tall + 2 * PAD
    lane = lax.broadcasted_iota(jnp.int32, (8, LANES), 1)
    sub = lax.broadcasted_iota(jnp.int32, (8, LANES), 0)
    on_top, on_bottom = sub == 0, sub == 7
    inner_low = lane >= samples
    inner_high = lane < LANES - samples

    def at(base, offset):
        return pl.ds(pl.multiple_of(base + offset, 8), 8)

    def bring(column, carry):
        for k, ref in enumerate((left_ref, low_ref, high_ref, right_ref)):
            base = (k * halo + column) * pitch
            noise[pl.ds(pl.multiple_of(base + PAD, 8), tall), :] = ref[column, 0:tall, :]
        betas[column] = spread_kappa(left_ref.at[column], tall, samples, segments)
        betas[column + halo] = beta_ref[column]
        betas[column + 2 * halo] = beta_ref[column + halo]
        betas[column + 3 * halo] = spread_kappa(right_ref.at[column], tall, samples, segments)
        return carry

    def bring_pair(pair, carry):
        return bring(2 * pair + 1, bring(2 * pair, carry))

    lax.fori_loop(0, halo // 2, bring_pair, 0)
    source = noise
    for turn in range(PASSES):
        target = (first_y, second_y)[turn % 2]
        level = PASSES - 1 - turn
        last = turn == PASSES - 1

        def sweep(column, count, source=source, target=target, level=level, last=last):
            base = column * pitch
            saved = [[] for _ in range(count)]
            for r in range(tall // 8):
                row = PAD + r * 8
                line = [source[at(base, t * pitch + row), :] for t in range(-1, count + 1)]
                for t in range(count):
                    north = source[pl.ds(base + (t * pitch + row - 1), 8), :]
                    south = source[pl.ds(base + (t * pitch + row + 1), 8), :]
                    if r == 0:
                        end = source[pl.ds(base + (t * pitch + PAD + tall - 1), 8), :]
                        end = jnp.where(inner_low, pltpu.roll(end, samples, 1), 0.0)
                        north = jnp.where(on_top, end, north)
                    if r == tall // 8 - 1:
                        end = source[pl.ds(base + (t * pitch + PAD - 7), 8), :]
                        end = jnp.where(inner_high, pltpu.roll(end, LANES - samples, 1), 0.0)
                        south = jnp.where(on_bottom, end, south)
                    beside = (north + south) + (line[t] + line[t + 2])
                    value = beside - betas[column + t, r * 8 : r * 8 + 8, :] * line[t + 1]
                    value = value + inner[level] * noise[at(base, t * pitch + row), :]
                    if last:
                        saved[t].append(value)
                    else:
                        target[at(base, t * pitch + row), :] = value
            for t in range(count if last else 0):
                own = column + t - halo
                turned = jnp.concatenate(saved[t], axis=0).T
                for i in range(segments):
                    lanes = slice(i * LANES, (i + 1) * LANES)
                    value = outer * turned[i * samples : (i + 1) * samples, :] + upd[own, :, lanes]
                    result[own, :, lanes] = value
                pltpu.make_async_copy(result.at[own], out_hbm.at[:, own, :], sem_out.at[own]).start()

        def step_wide(step, carry, sweep=sweep, turn=turn):
            sweep(turn + 1 + WIDE * step, WIDE)
            return carry

        count = columns - 2 * (turn + 1)
        lax.fori_loop(0, count // WIDE, step_wide, 0)
        if count % WIDE:
            sweep(jnp.int32(turn + 1 + count - count % WIDE), count % WIDE)
        source = target
    for column in range(width):
        pltpu.make_async_copy(result.at[column], out_hbm.at[:, column, :], sem_out.at[column]).wait()


def shift_to(value, axis, steps):
    count = lax.axis_size(axis)
    return lax.ppermute(value, axis, [(source, (source + steps) % count) for source in range(count)])


def local(white_noise, kappa_sq, station_lat, station_lon, station_weights, station_count):
    samples, width, height = white_noise.shape
    slots = station_lat.shape[0]
    halo = PASSES
    anywhere = pl.BlockSpec(memory_space=pl.ANY)
    whole = pl.BlockSpec(memory_space=pltpu.VMEM)
    hbm = pl.BlockSpec(memory_space=pltpu.HBM)

    def in_hbm(items):
        return [pltpu.with_memory_space_constraint(item, pltpu.HBM) for item in items]

    pack = pl.pallas_call(
        lambda *refs: pack_kernel(*refs, samples=samples, slots=slots),
        out_shape=pltpu.VMEM((samples + 2, slots), jnp.float32),
        in_specs=[hbm] * 3 + [pl.BlockSpec(memory_space=pltpu.SMEM)],
        out_specs=whole,
        scratch_shapes=[pltpu.VMEM((1, slots), jnp.float32), pltpu.SemaphoreType.DMA((3,))],
        compiler_params=pltpu.CompilerParams(vmem_limit_bytes=ROOM),
        name="pack",
    )(*in_hbm((station_lat[None], station_lon[None], station_weights)), station_count)
    later = lax.optimization_barrier((pack, white_noise, kappa_sq))
    pack = later[0]
    packs = []
    for step in range(-HOPS, HOPS + 1):
        packs.append(pack if step == 0 else shift_to(pack, "lon", -step))

    segments = height // LANES
    tall = height * samples // LANES
    half = pltpu.VMEM((halo, tall + segments, LANES), jnp.float32)
    low, high, beta = pl.pallas_call(
        lambda *refs: turn_kernel(*refs, samples=samples, width=width, height=height),
        out_shape=(half, half, pltpu.VMEM((width, tall, LANES), jnp.float32)),
        in_specs=[hbm] * 2,
        out_specs=(whole, whole, whole),
        scratch_shapes=[
            pltpu.VMEM((width, samples, height), jnp.float32),
            pltpu.VMEM((width, height), jnp.float32),
            pltpu.SemaphoreType.DMA((width,)),
            pltpu.SemaphoreType.DMA,
        ],
        compiler_params=pltpu.CompilerParams(vmem_limit_bytes=ROOM),
        name="turn",
    )(*in_hbm(later[1:]))
    left = shift_to(high, "lon", 1)
    right = shift_to(low, "lon", -1)
    packs = [pltpu.with_memory_space_constraint(item, pltpu.VMEM) for item in packs]

    lists = 2 * HOPS + 1
    band = HOPS * width
    bands = height // band
    rows_m = (bands + 1 + 7) // 8 * 8
    room = lists * slots + 2 * LANES
    upd = pl.pallas_call(
        lambda *refs: station_kernel(*refs, samples=samples, width=width, height=height, slots=slots),
        out_shape=pltpu.VMEM((width, samples, height), jnp.float32),
        in_specs=[whole] * lists,
        out_specs=whole,
        scratch_shapes=[
            pltpu.VMEM((8, lists * rows_m), jnp.int32),
            pltpu.SMEM((8, lists * rows_m), jnp.int32),
            pltpu.VMEM((lists, LANES, slots), jnp.bfloat16),
            pltpu.VMEM((room, LANES), jnp.float32),
            pltpu.VMEM((room, LANES), jnp.float32),
            pltpu.VMEM((room // CH, samples, 3 * CH), jnp.bfloat16),
            pltpu.VMEM((room, LANES), jnp.float32),
            pltpu.VMEM((room, band * width), jnp.float32),
            pltpu.VMEM((bands + 1, samples, band * width), jnp.float32),
            pltpu.SMEM((bands + 1,), jnp.int32),
            pltpu.SemaphoreType.DMA,
        ],
        compiler_params=pltpu.CompilerParams(vmem_limit_bytes=ROOM),
        cost_estimate=pl.CostEstimate(flops=10000000000, transcendentals=10**7, bytes_accessed=2 * 10**6),
        name="stations",
    )(*packs)
    columns = width + 2 * halo
    field = pltpu.VMEM(((columns + 2) * (tall + 2 * PAD), LANES), jnp.float32)
    fields = [left, low, high, right, beta, upd]
    fields = [pltpu.with_memory_space_constraint(item, pltpu.VMEM) for item in fields]
    return pl.pallas_call(
        lambda *refs: prior_kernel(*refs, samples=samples, width=width, height=height),
        out_shape=jax.ShapeDtypeStruct((samples, width, height), jnp.float32),
        in_specs=[whole] * 6,
        out_specs=anywhere,
        scratch_shapes=[
            field,
            pltpu.VMEM((columns + 2, tall, LANES), jnp.float32),
            field,
            field,
            pltpu.VMEM((width, samples, height), jnp.float32),
            pltpu.SemaphoreType.DMA((width,)),
        ],
        compiler_params=pltpu.CompilerParams(vmem_limit_bytes=ROOM),
        name="prior",
    )(*fields)


def solution(mesh):
    in_specs = (
        P("groups", "lon", None),
        P("lon", None),
        P(("groups", "lon")),
        P(("groups", "lon")),
        P("groups", "lon"),
        P(("groups", "lon")),
    )
    out_specs = P("groups", "lon", None)
    return jax.shard_map(local, mesh=mesh, in_specs=in_specs, out_specs=out_specs, check_vma=False)
```

```python
import math

import jax
import jax.numpy as jnp
import numpy as np
from jax import lax
from jax.experimental import pallas as pl
from jax.experimental.pallas import tpu as pltpu
from jax.sharding import PartitionSpec as P

PASSES = 8
HOPS = 2
CHEB = (0.62, -0.41, 0.3, -0.22, 0.16, -0.115, 0.08, -0.055, 0.04)
LOG2E = math.log2(math.e)
FAR = 4096.0
CH = 32
UNROLL = 32
LANES = 128
BLOCK = 128
ROOM = 24 * 2**20
PAD = 8
WIDE = 8


def horner_coeffs():
    powers = np.polynomial.chebyshev.cheb2poly(np.array(CHEB))
    lead = powers[PASSES]
    inner = [float(powers[k] / lead * (-4.5) ** (PASSES - k)) for k in range(PASSES)]
    return inner, float(lead / 4.5**PASSES)


def split3(value):
    high = value.astype(jnp.bfloat16)
    rest = value - high.astype(jnp.float32)
    middle = rest.astype(jnp.bfloat16)
    low = (rest - middle.astype(jnp.float32)).astype(jnp.bfloat16)
    return high, middle, low


def station_kernel(
    p0, p1, p2, p3, p4, out_ref,
    table_v, table_s, data, sorted_s, merged, wts, latb, dlon2, stage, starts, sem_s,
    *, samples, width, height, slots,
):
    packs = (p0, p1, p2, p3, p4)
    lists = len(packs)
    radius = float(HOPS * width)
    band = int(radius)
    bands = height // band
    rows_m = (bands + 1 + 7) // 8 * 8
    scale = LOG2E / radius
    groups = band * width // LANES
    per_group = LANES // band
    index_m = lax.broadcasted_iota(jnp.int32, (rows_m, slots), 0).astype(jnp.float32)
    equal, below, onehot = [], [], []
    for pack in packs:
        lat = pack[samples : samples + 1, :]
        bucket = jnp.minimum(jnp.floor(lat * (1.0 / radius)), float(bands - 1))
        bucket = jnp.where(lat > FAR * 0.5, float(bands), bucket)
        bucket = jnp.broadcast_to(bucket, (rows_m, slots))
        equal.append(jnp.where(bucket == index_m, 1.0, 0.0))
        below.append(jnp.where(bucket < index_m, 1.0, 0.0).astype(jnp.bfloat16))
    before = lax.broadcasted_iota(jnp.int32, (slots, slots), 0) < lax.broadcasted_iota(
        jnp.int32, (slots, slots), 1
    )
    before = jnp.where(before, 1.0, 0.0).astype(jnp.bfloat16)
    all_below = jnp.concatenate(below, axis=0)
    inside = jnp.dot(
        jnp.concatenate(equal, axis=0).astype(jnp.bfloat16), before, preferred_element_type=jnp.float32
    )
    base = jnp.dot(all_below, jnp.ones((slots, LANES), jnp.bfloat16), preferred_element_type=jnp.float32)
    counts = lax.dot_general(
        jnp.ones((8, slots), jnp.bfloat16), all_below, (((1,), (1,)), ((), ())),
        preferred_element_type=jnp.float32,
    )
    table_v[...] = counts.astype(jnp.int32)
    copy = pltpu.make_async_copy(table_v, table_s, sem_s)
    copy.start()
    ranks = []
    for index in range(lists):
        rows = slice(index * rows_m, (index + 1) * rows_m)
        start = base[rows]
        start = jnp.concatenate([start] * (slots // LANES), axis=1)
        ranks.append(jnp.sum(equal[index] * (inside[rows] + start), axis=0, keepdims=True))

    factor = 4.0 * math.exp(-1.0) / LOG2E**5
    for index, pack in enumerate(packs):
        weights = pack[0:samples, :] * factor
        w_high = weights.astype(jnp.bfloat16)
        w_low = (weights - w_high.astype(jnp.float32)).astype(jnp.bfloat16)
        lat = pack[samples : samples + 1, :]
        lon = pack[samples + 1 : samples + 2, :] + float((index - HOPS) * width)
        parts = split3(lat) + split3(lon)
        parts = [part.astype(jnp.float32) for part in parts]
        filler = jnp.zeros((LANES - 2 * samples - 6, slots), jnp.float32)
        block = jnp.concatenate(
            [w_high.astype(jnp.float32), w_low.astype(jnp.float32)] + parts + [filler], axis=0
        )
        data[index] = block.astype(jnp.bfloat16)

    for m in range(bands + 1):
        stage[m] = jnp.zeros((samples, groups * LANES), jnp.float32)
    copy.wait()

    row_p = lax.broadcasted_iota(jnp.int32, (LANES, slots), 0).astype(jnp.float32)
    longest = table_s[0, bands]
    for index in range(1, lists):
        longest = jnp.maximum(longest, table_s[0, index * rows_m + bands])

    def sort_block(block, carry):
        first = block * LANES
        for index in range(lists):
            pick = ranks[index] - first.astype(jnp.float32)
            pick = jnp.where(jnp.broadcast_to(pick, (LANES, slots)) == row_p, 1.0, 0.0)
            moved = lax.dot_general(
                pick.astype(jnp.bfloat16), data[index], (((1,), (1,)), ((), ())),
                preferred_element_type=jnp.float32,
            )
            sorted_s[pl.ds(pl.multiple_of(index * slots + first, LANES), LANES), :] = moved
        return carry

    def sort_pair(pair, carry):
        return sort_block(2 * pair + 1, sort_block(2 * pair, carry))

    lax.fori_loop(0, (longest + 2 * LANES - 1) // (2 * LANES), sort_pair, 0)

    step = 32

    def merge_band(m, position):
        starts[m] = position
        begins, sizes, places = [], [], []
        for index in range(lists):
            begin = table_s[0, index * rows_m + m]
            sizes.append(table_s[0, index * rows_m + m + 1] - begin)
            begins.append(index * slots + begin)
            places.append(position)
            position = position + sizes[-1]
        for index in range(lists):
            merged[pl.ds(places[index], step), :] = sorted_s[pl.ds(begins[index], step), :]
        largest = sizes[0]
        for size in sizes[1:]:
            largest = jnp.maximum(largest, size)

        @pl.when(largest > step)
        def _():
            for index in range(lists):

                def more(k, carry, index=index):
                    rows = sorted_s[pl.ds(begins[index] + k * step, step), :]
                    merged[pl.ds(places[index] + k * step, step), :] = rows
                    return carry

                lax.fori_loop(0, (sizes[index] + step - 1) // step, more, 0)

        return position

    def merge_pair(pair, position):
        return merge_band(2 * pair + 1, merge_band(2 * pair, position))

    total = lax.fori_loop(0, bands // 2, merge_pair, jnp.int32(0))
    starts[bands] = total
    lane = lax.broadcasted_iota(jnp.int32, (BLOCK, LANES), 1)
    merged[pl.ds(total, BLOCK), :] = jnp.where(lane == 2 * samples, FAR, 0.0)

    lane_row = lax.broadcasted_iota(jnp.int32, (1, LANES), 1)
    cell_in = (lane_row % band).astype(jnp.float32)
    cell_lon = (lane_row // band).astype(jnp.float32)

    row_of = lax.broadcasted_iota(jnp.int32, (LANES, 2 * LANES), 0) - 2 * samples
    part_of = lax.broadcasted_iota(jnp.int32, (LANES, 2 * LANES), 1) // LANES * 3
    gather = jnp.where((row_of >= part_of) & (row_of < part_of + 3), 1.0, 0.0).astype(jnp.bfloat16)
    turn_rows = lax.broadcasted_iota(jnp.int32, (samples, LANES), 0)
    turn_lanes = lax.broadcasted_iota(jnp.int32, (samples, LANES), 1)
    select = (turn_lanes == turn_rows) | (turn_lanes == turn_rows + samples)
    select = jnp.where(select, 1.0, 0.0).astype(jnp.bfloat16)
    is_high = lax.broadcasted_iota(jnp.int32, (CH, LANES), 1) < samples

    def prepare_pair(pair, carry):
        for half in range(2):
            prepare(2 * pair + half)
        return carry

    def prepare(block):
        first = pl.multiple_of(block * BLOCK, BLOCK)
        rows = merged[pl.ds(first, BLOCK), :]
        places = jnp.dot(rows.astype(jnp.bfloat16), gather, preferred_element_type=jnp.float32)
        latb[pl.ds(first, BLOCK), :] = places[:, 0:LANES]
        lon = places[:, LANES : 2 * LANES]
        for group in range(groups):
            offset = (lon - (cell_lon + float(group * per_group))) * scale
            dlon2[pl.ds(first, BLOCK), group * LANES : (group + 1) * LANES] = offset * offset + 1e-30
        for k in range(BLOCK // CH):
            some = rows[k * CH : (k + 1) * CH, :]
            high_rows = jnp.where(is_high, some, 0.0)
            low_rows = jnp.where(is_high, 0.0, some)
            thrice = jnp.concatenate([high_rows, high_rows, low_rows], axis=0).astype(jnp.bfloat16)
            turned = lax.dot_general(
                select, thrice, (((1,), (1,)), ((), ())), preferred_element_type=jnp.float32
            )
            wts[block * (BLOCK // CH) + k] = turned.astype(jnp.bfloat16)

    lax.fori_loop(0, total // (2 * BLOCK) + 1, prepare_pair, 0)

    def low_of(m):
        return starts[jnp.maximum(m - 1, 0)] // CH

    def high_of(m):
        return jnp.maximum((starts[jnp.minimum(m + 2, bands)] + CH - 1) // CH, low_of(m) + 1)

    def eval_items(carry):
        m, chunk = carry
        for _ in range(UNROLL):
            first = pl.multiple_of(chunk * CH, CH)
            offset = (latb[pl.ds(first, CH), :] - (cell_in + (m * band).astype(jnp.float32))) * scale
            offset = offset * offset
            kerns = []
            for group in range(groups):
                square = offset + dlon2[pl.ds(first, CH), group * LANES : (group + 1) * LANES]
                taper = jnp.maximum(LOG2E - square * lax.rsqrt(square), 0.0)
                twice = taper * taper
                kerns.append((twice * twice) * (1.25 * LOG2E - taper) * jnp.exp2(taper))
            kern = jnp.concatenate(kerns, axis=1)
            high_part = kern.astype(jnp.bfloat16)
            low_part = (kern - high_part.astype(jnp.float32)).astype(jnp.bfloat16)
            parts = jnp.concatenate([high_part, low_part, high_part], axis=0)
            stage[m] += jnp.dot(wts[chunk], parts, preferred_element_type=jnp.float32)
            done = chunk + 1 >= high_of(m)
            after = jnp.minimum(m + 1, bands)
            chunk = jnp.where(done, low_of(after), chunk + 1)
            chunk = jnp.where(after == bands, jnp.where(done, 0, chunk), chunk)
            m = jnp.where(done, after, m)
        return m, chunk

    first_item = (jnp.int32(0), low_of(jnp.int32(0)))
    lax.while_loop(lambda carry: carry[0] < bands, eval_items, first_item)

    part = lax.broadcasted_iota(jnp.int32, (samples, LANES), 1) // band

    def lay_out_pair(pair, carry):
        for half in range(2):
            lay_out(2 * pair + half)
        return carry

    def lay_out(block):
        at = pl.multiple_of(block * LANES, LANES)
        for group in range(groups):
            pieces = [
                stage[block * per_group + j, :, group * LANES : (group + 1) * LANES]
                for j in range(per_group)
            ]
            bit = 1
            while bit < per_group:
                keep = (part & bit) == 0
                for j in range(per_group):
                    if j & bit == 0:
                        first, second = pieces[j], pieces[j | bit]
                        pieces[j] = jnp.where(keep, first, pltpu.roll(second, bit * band, 1))
                        pieces[j | bit] = jnp.where(keep, pltpu.roll(first, LANES - bit * band, 1), second)
                bit *= 2
            for j in range(per_group):
                out_ref[group * per_group + j, :, pl.ds(at, LANES)] = pieces[j]

    lax.fori_loop(0, height // (2 * LANES), lay_out_pair, 0)


def pack_kernel(lat_hbm, lon_hbm, weights_hbm, count_ref, pack_ref, lat, sems, *, samples, slots):
    copies = [
        pltpu.make_async_copy(lat_hbm, lat, sems.at[0]),
        pltpu.make_async_copy(lon_hbm, pack_ref.at[samples + 1 : samples + 2], sems.at[1]),
        pltpu.make_async_copy(weights_hbm, pack_ref.at[0:samples], sems.at[2]),
    ]
    for copy in copies:
        copy.start()
    for copy in copies:
        copy.wait()
    slot = lax.broadcasted_iota(jnp.int32, (1, slots), 1)
    pack_ref[samples : samples + 1, :] = jnp.where(slot < count_ref[0], lat[...], FAR)


def turn_kernel(
    x_hbm, kappa_hbm, low_ref, high_ref, beta_ref, noise, kap, sem_x, sem_k, *, samples, width, height
):
    segments = height // LANES
    tall = height * samples // LANES
    copies = [pltpu.make_async_copy(x_hbm.at[:, c, :], noise.at[c], sem_x.at[c]) for c in range(width)]
    copies.append(pltpu.make_async_copy(kappa_hbm, kap, sem_k))
    for copy in copies:
        copy.start()
    copies[-1].wait()
    for column in range(width):
        half = (low_ref, high_ref)[column // PASSES]
        for i in range(segments):
            piece = kap[column : column + 1, i * LANES : (i + 1) * LANES]
            half[column % PASSES, tall + i : tall + i + 1, :] = piece
        beta_ref[column] = spread_kappa(half.at[column % PASSES], tall, samples, segments)
    for column in range(width):
        copies[column].wait()
    for column in range(width):
        half = (low_ref, high_ref)[column // PASSES]
        pieces = [noise[column, :, i * LANES : (i + 1) * LANES] for i in range(segments)]
        half[column % PASSES, 0:tall, :] = jnp.concatenate(pieces, axis=0).T


def spread_kappa(ref, start, samples, segments):
    rows = [ref[start + i : start + i + 1, :] - 0.5 for i in range(segments)]
    rows = [jnp.broadcast_to(row, (samples, LANES)) for row in rows]
    return jnp.concatenate(rows, axis=0).T


def prior_kernel(
    left_ref, low_ref, high_ref, right_ref, beta_ref, upd, out_hbm,
    noise, betas, first_y, second_y, result, sem_out, *, samples, width, height,
):
    halo = PASSES
    inner, outer = horner_coeffs()
    segments = height // LANES
    tall = height * samples // LANES
    columns = width + 2 * halo
    pitch = tall + 2 * PAD
    lane = lax.broadcasted_iota(jnp.int32, (8, LANES), 1)
    sub = lax.broadcasted_iota(jnp.int32, (8, LANES), 0)
    on_top, on_bottom = sub == 0, sub == 7
    inner_low = lane >= samples
    inner_high = lane < LANES - samples

    def at(base, offset):
        return pl.ds(pl.multiple_of(base + offset, 8), 8)

    def bring(column, carry):
        for k, ref in enumerate((left_ref, low_ref, high_ref, right_ref)):
            base = (k * halo + column) * pitch
            noise[pl.ds(pl.multiple_of(base + PAD, 8), tall), :] = ref[column, 0:tall, :]
        betas[column] = spread_kappa(left_ref.at[column], tall, samples, segments)
        betas[column + halo] = beta_ref[column]
        betas[column + 2 * halo] = beta_ref[column + halo]
        betas[column + 3 * halo] = spread_kappa(right_ref.at[column], tall, samples, segments)
        return carry

    def bring_four(four, carry):
        for k in range(4):
            bring(4 * four + k, carry)
        return carry

    lax.fori_loop(0, halo // 4, bring_four, 0)
    source = noise
    for turn in range(PASSES):
        target = (first_y, second_y)[turn % 2]
        level = PASSES - 1 - turn
        last = turn == PASSES - 1

        def sweep(column, count, source=source, target=target, level=level, last=last):
            base = column * pitch
            saved = [[] for _ in range(count)]
            for r in range(tall // 8):
                row = PAD + r * 8
                line = [source[at(base, t * pitch + row), :] for t in range(-1, count + 1)]
                for t in range(count):
                    north = source[pl.ds(base + (t * pitch + row - 1), 8), :]
                    south = source[pl.ds(base + (t * pitch + row + 1), 8), :]
                    if r == 0:
                        end = source[pl.ds(base + (t * pitch + PAD + tall - 1), 8), :]
                        end = jnp.where(inner_low, pltpu.roll(end, samples, 1), 0.0)
                        north = jnp.where(on_top, end, north)
                    if r == tall // 8 - 1:
                        end = source[pl.ds(base + (t * pitch + PAD - 7), 8), :]
                        end = jnp.where(inner_high, pltpu.roll(end, LANES - samples, 1), 0.0)
                        south = jnp.where(on_bottom, end, south)
                    beside = (north + south) + (line[t] + line[t + 2])
                    value = beside - betas[column + t, r * 8 : r * 8 + 8, :] * line[t + 1]
                    value = value + inner[level] * noise[at(base, t * pitch + row), :]
                    if last:
                        saved[t].append(value)
                    else:
                        target[at(base, t * pitch + row), :] = value
            for t in range(count if last else 0):
                own = column + t - halo
                turned = jnp.concatenate(saved[t], axis=0).T
                for i in range(segments):
                    lanes = slice(i * LANES, (i + 1) * LANES)
                    value = outer * turned[i * samples : (i + 1) * samples, :] + upd[own, :, lanes]
                    result[own, :, lanes] = value
                pltpu.make_async_copy(result.at[own], out_hbm.at[:, own, :], sem_out.at[own]).start()

        def step_wide(step, carry, sweep=sweep, turn=turn):
            sweep(turn + 1 + WIDE * step, WIDE)
            return carry

        count = columns - 2 * (turn + 1)
        lax.fori_loop(0, count // WIDE, step_wide, 0)
        if count % WIDE:
            sweep(jnp.int32(turn + 1 + count - count % WIDE), count % WIDE)
        source = target
    for column in range(width):
        pltpu.make_async_copy(result.at[column], out_hbm.at[:, column, :], sem_out.at[column]).wait()


def shift_to(value, axis, steps):
    count = lax.axis_size(axis)
    return lax.ppermute(value, axis, [(source, (source + steps) % count) for source in range(count)])


def local(white_noise, kappa_sq, station_lat, station_lon, station_weights, station_count):
    samples, width, height = white_noise.shape
    slots = station_lat.shape[0]
    halo = PASSES
    anywhere = pl.BlockSpec(memory_space=pl.ANY)
    whole = pl.BlockSpec(memory_space=pltpu.VMEM)
    hbm = pl.BlockSpec(memory_space=pltpu.HBM)

    def in_hbm(items):
        return [pltpu.with_memory_space_constraint(item, pltpu.HBM) for item in items]

    pack = pl.pallas_call(
        lambda *refs: pack_kernel(*refs, samples=samples, slots=slots),
        out_shape=pltpu.VMEM((samples + 2, slots), jnp.float32),
        in_specs=[hbm] * 3 + [pl.BlockSpec(memory_space=pltpu.SMEM)],
        out_specs=whole,
        scratch_shapes=[pltpu.VMEM((1, slots), jnp.float32), pltpu.SemaphoreType.DMA((3,))],
        compiler_params=pltpu.CompilerParams(vmem_limit_bytes=ROOM),
        name="pack",
    )(*in_hbm((station_lat[None], station_lon[None], station_weights)), station_count)
    later = lax.optimization_barrier((pack, white_noise, kappa_sq))
    pack = later[0]
    packs = []
    for step in range(-HOPS, HOPS + 1):
        packs.append(pack if step == 0 else shift_to(pack, "lon", -step))

    segments = height // LANES
    tall = height * samples // LANES
    half = pltpu.VMEM((halo, tall + segments, LANES), jnp.float32)
    low, high, beta = pl.pallas_call(
        lambda *refs: turn_kernel(*refs, samples=samples, width=width, height=height),
        out_shape=(half, half, pltpu.VMEM((width, tall, LANES), jnp.float32)),
        in_specs=[hbm] * 2,
        out_specs=(whole, whole, whole),
        scratch_shapes=[
            pltpu.VMEM((width, samples, height), jnp.float32),
            pltpu.VMEM((width, height), jnp.float32),
            pltpu.SemaphoreType.DMA((width,)),
            pltpu.SemaphoreType.DMA,
        ],
        compiler_params=pltpu.CompilerParams(vmem_limit_bytes=ROOM),
        name="turn",
    )(*in_hbm(later[1:]))
    left = shift_to(high, "lon", 1)
    right = shift_to(low, "lon", -1)
    packs = [pltpu.with_memory_space_constraint(item, pltpu.VMEM) for item in packs]

    lists = 2 * HOPS + 1
    band = HOPS * width
    bands = height // band
    rows_m = (bands + 1 + 7) // 8 * 8
    room = lists * slots + 2 * LANES
    upd = pl.pallas_call(
        lambda *refs: station_kernel(*refs, samples=samples, width=width, height=height, slots=slots),
        out_shape=pltpu.VMEM((width, samples, height), jnp.float32),
        in_specs=[whole] * lists,
        out_specs=whole,
        scratch_shapes=[
            pltpu.VMEM((8, lists * rows_m), jnp.int32),
            pltpu.SMEM((8, lists * rows_m), jnp.int32),
            pltpu.VMEM((lists, LANES, slots), jnp.bfloat16),
            pltpu.VMEM((room, LANES), jnp.float32),
            pltpu.VMEM((room, LANES), jnp.float32),
            pltpu.VMEM((room // CH, samples, 3 * CH), jnp.bfloat16),
            pltpu.VMEM((room, LANES), jnp.float32),
            pltpu.VMEM((room, band * width), jnp.float32),
            pltpu.VMEM((bands + 1, samples, band * width), jnp.float32),
            pltpu.SMEM((bands + 1,), jnp.int32),
            pltpu.SemaphoreType.DMA,
        ],
        compiler_params=pltpu.CompilerParams(vmem_limit_bytes=ROOM),
        cost_estimate=pl.CostEstimate(flops=10000000000, transcendentals=10**7, bytes_accessed=2 * 10**6),
        name="stations",
    )(*packs)
    columns = width + 2 * halo
    field = pltpu.VMEM(((columns + 2) * (tall + 2 * PAD), LANES), jnp.float32)
    fields = [left, low, high, right, beta, upd]
    fields = [pltpu.with_memory_space_constraint(item, pltpu.VMEM) for item in fields]
    return pl.pallas_call(
        lambda *refs: prior_kernel(*refs, samples=samples, width=width, height=height),
        out_shape=jax.ShapeDtypeStruct((samples, width, height), jnp.float32),
        in_specs=[whole] * 6,
        out_specs=anywhere,
        scratch_shapes=[
            field,
            pltpu.VMEM((columns + 2, tall, LANES), jnp.float32),
            field,
            field,
            pltpu.VMEM((width, samples, height), jnp.float32),
            pltpu.SemaphoreType.DMA((width,)),
        ],
        compiler_params=pltpu.CompilerParams(vmem_limit_bytes=ROOM),
        name="prior",
    )(*fields)


def solution(mesh):
    in_specs = (
        P("groups", "lon", None),
        P("lon", None),
        P(("groups", "lon")),
        P(("groups", "lon")),
        P("groups", "lon"),
        P(("groups", "lon")),
    )
    out_specs = P("groups", "lon", None)
    return jax.shard_map(local, mesh=mesh, in_specs=in_specs, out_specs=out_specs, check_vma=False)
```

```python
import math

import jax
import jax.numpy as jnp
import numpy as np
from jax import lax
from jax.experimental import pallas as pl
from jax.experimental.pallas import tpu as pltpu
from jax.sharding import PartitionSpec as P

PASSES = 8
HOPS = 2
CHEB = (0.62, -0.41, 0.3, -0.22, 0.16, -0.115, 0.08, -0.055, 0.04)
LOG2E = math.log2(math.e)
FAR = 4096.0
CH = 32
UNROLL = 24
LANES = 128
BLOCK = 128
ROOM = 24 * 2**20
PAD = 8
WIDE = 8


def horner_coeffs():
    powers = np.polynomial.chebyshev.cheb2poly(np.array(CHEB))
    lead = powers[PASSES]
    inner = [float(powers[k] / lead * (-4.5) ** (PASSES - k)) for k in range(PASSES)]
    return inner, float(lead / 4.5**PASSES)


def split3(value):
    high = value.astype(jnp.bfloat16)
    rest = value - high.astype(jnp.float32)
    middle = rest.astype(jnp.bfloat16)
    low = (rest - middle.astype(jnp.float32)).astype(jnp.bfloat16)
    return high, middle, low


def station_kernel(
    p0, p1, p2, p3, p4, out_ref,
    table_v, table_s, data, sorted_s, merged, wts, latb, dlon2, stage, starts, sem_s,
    *, samples, width, height, slots,
):
    packs = (p0, p1, p2, p3, p4)
    lists = len(packs)
    radius = float(HOPS * width)
    band = int(radius)
    bands = height // band
    rows_m = (bands + 1 + 7) // 8 * 8
    scale = LOG2E / radius
    groups = band * width // LANES
    per_group = LANES // band
    index_m = lax.broadcasted_iota(jnp.int32, (rows_m, slots), 0).astype(jnp.float32)
    equal, below, onehot = [], [], []
    for pack in packs:
        lat = pack[samples : samples + 1, :]
        bucket = jnp.minimum(jnp.floor(lat * (1.0 / radius)), float(bands - 1))
        bucket = jnp.where(lat > FAR * 0.5, float(bands), bucket)
        bucket = jnp.broadcast_to(bucket, (rows_m, slots))
        equal.append(jnp.where(bucket == index_m, 1.0, 0.0))
        below.append(jnp.where(bucket < index_m, 1.0, 0.0).astype(jnp.bfloat16))
    before = lax.broadcasted_iota(jnp.int32, (slots, slots), 0) < lax.broadcasted_iota(
        jnp.int32, (slots, slots), 1
    )
    before = jnp.where(before, 1.0, 0.0).astype(jnp.bfloat16)
    all_below = jnp.concatenate(below, axis=0)
    inside = jnp.dot(
        jnp.concatenate(equal, axis=0).astype(jnp.bfloat16), before, preferred_element_type=jnp.float32
    )
    base = jnp.dot(all_below, jnp.ones((slots, LANES), jnp.bfloat16), preferred_element_type=jnp.float32)
    counts = lax.dot_general(
        jnp.ones((8, slots), jnp.bfloat16), all_below, (((1,), (1,)), ((), ())),
        preferred_element_type=jnp.float32,
    )
    table_v[...] = counts.astype(jnp.int32)
    copy = pltpu.make_async_copy(table_v, table_s, sem_s)
    copy.start()
    ranks = []
    for index in range(lists):
        rows = slice(index * rows_m, (index + 1) * rows_m)
        start = base[rows]
        start = jnp.concatenate([start] * (slots // LANES), axis=1)
        ranks.append(jnp.sum(equal[index] * (inside[rows] + start), axis=0, keepdims=True))

    factor = 4.0 * math.exp(-1.0) / LOG2E**5
    for index, pack in enumerate(packs):
        weights = pack[0:samples, :] * factor
        w_high = weights.astype(jnp.bfloat16)
        w_low = (weights - w_high.astype(jnp.float32)).astype(jnp.bfloat16)
        lat = pack[samples : samples + 1, :]
        lon = pack[samples + 1 : samples + 2, :] + float((index - HOPS) * width)
        parts = split3(lat) + split3(lon)
        parts = [part.astype(jnp.float32) for part in parts]
        filler = jnp.zeros((LANES - 2 * samples - 6, slots), jnp.float32)
        block = jnp.concatenate(
            [w_high.astype(jnp.float32), w_low.astype(jnp.float32)] + parts + [filler], axis=0
        )
        data[index] = block.astype(jnp.bfloat16)

    for m in range(bands + 1):
        stage[m] = jnp.zeros((samples, groups * LANES), jnp.float32)
    copy.wait()

    row_p = lax.broadcasted_iota(jnp.int32, (LANES, slots), 0).astype(jnp.float32)
    longest = table_s[0, bands]
    for index in range(1, lists):
        longest = jnp.maximum(longest, table_s[0, index * rows_m + bands])

    def sort_block(block, carry):
        first = block * LANES
        for index in range(lists):
            pick = ranks[index] - first.astype(jnp.float32)
            pick = jnp.where(jnp.broadcast_to(pick, (LANES, slots)) == row_p, 1.0, 0.0)
            moved = lax.dot_general(
                pick.astype(jnp.bfloat16), data[index], (((1,), (1,)), ((), ())),
                preferred_element_type=jnp.float32,
            )
            sorted_s[pl.ds(pl.multiple_of(index * slots + first, LANES), LANES), :] = moved
        return carry

    def sort_pair(pair, carry):
        return sort_block(2 * pair + 1, sort_block(2 * pair, carry))

    lax.fori_loop(0, (longest + 2 * LANES - 1) // (2 * LANES), sort_pair, 0)

    step = 32

    def merge_band(m, position):
        starts[m] = position
        begins, sizes, places = [], [], []
        for index in range(lists):
            begin = table_s[0, index * rows_m + m]
            sizes.append(table_s[0, index * rows_m + m + 1] - begin)
            begins.append(index * slots + begin)
            places.append(position)
            position = position + sizes[-1]
        for index in range(lists):
            merged[pl.ds(places[index], step), :] = sorted_s[pl.ds(begins[index], step), :]
        largest = sizes[0]
        for size in sizes[1:]:
            largest = jnp.maximum(largest, size)

        @pl.when(largest > step)
        def _():
            for index in range(lists):

                def more(k, carry, index=index):
                    rows = sorted_s[pl.ds(begins[index] + k * step, step), :]
                    merged[pl.ds(places[index] + k * step, step), :] = rows
                    return carry

                lax.fori_loop(0, (sizes[index] + step - 1) // step, more, 0)

        return position

    def merge_pair(pair, position):
        return merge_band(2 * pair + 1, merge_band(2 * pair, position))

    total = lax.fori_loop(0, bands // 2, merge_pair, jnp.int32(0))
    starts[bands] = total
    lane = lax.broadcasted_iota(jnp.int32, (BLOCK, LANES), 1)
    merged[pl.ds(total, BLOCK), :] = jnp.where(lane == 2 * samples, FAR, 0.0)

    lane_row = lax.broadcasted_iota(jnp.int32, (1, LANES), 1)
    cell_in = (lane_row % band).astype(jnp.float32)
    cell_lon = (lane_row // band).astype(jnp.float32)

    row_of = lax.broadcasted_iota(jnp.int32, (LANES, 2 * LANES), 0) - 2 * samples
    part_of = lax.broadcasted_iota(jnp.int32, (LANES, 2 * LANES), 1) // LANES * 3
    gather = jnp.where((row_of >= part_of) & (row_of < part_of + 3), 1.0, 0.0).astype(jnp.bfloat16)
    turn_rows = lax.broadcasted_iota(jnp.int32, (samples, LANES), 0)
    turn_lanes = lax.broadcasted_iota(jnp.int32, (samples, LANES), 1)
    select = (turn_lanes == turn_rows) | (turn_lanes == turn_rows + samples)
    select = jnp.where(select, 1.0, 0.0).astype(jnp.bfloat16)
    is_high = lax.broadcasted_iota(jnp.int32, (CH, LANES), 1) < samples

    def prepare_pair(pair, carry):
        for half in range(2):
            prepare(2 * pair + half)
        return carry

    def prepare(block):
        first = pl.multiple_of(block * BLOCK, BLOCK)
        rows = merged[pl.ds(first, BLOCK), :]
        places = jnp.dot(rows.astype(jnp.bfloat16), gather, preferred_element_type=jnp.float32)
        latb[pl.ds(first, BLOCK), :] = places[:, 0:LANES]
        lon = places[:, LANES : 2 * LANES]
        for group in range(groups):
            offset = (lon - (cell_lon + float(group * per_group))) * scale
            dlon2[pl.ds(first, BLOCK), group * LANES : (group + 1) * LANES] = offset * offset + 1e-30
        for k in range(BLOCK // CH):
            some = rows[k * CH : (k + 1) * CH, :]
            high_rows = jnp.where(is_high, some, 0.0)
            low_rows = jnp.where(is_high, 0.0, some)
            thrice = jnp.concatenate([high_rows, high_rows, low_rows], axis=0).astype(jnp.bfloat16)
            turned = lax.dot_general(
                select, thrice, (((1,), (1,)), ((), ())), preferred_element_type=jnp.float32
            )
            wts[block * (BLOCK // CH) + k] = turned.astype(jnp.bfloat16)

    lax.fori_loop(0, total // (2 * BLOCK) + 1, prepare_pair, 0)

    def low_of(m):
        return starts[jnp.maximum(m - 1, 0)] // CH

    def high_of(m):
        return jnp.maximum((starts[jnp.minimum(m + 2, bands)] + CH - 1) // CH, low_of(m) + 1)

    def eval_items(carry):
        m, chunk = carry
        for _ in range(UNROLL):
            first = pl.multiple_of(chunk * CH, CH)
            offset = (latb[pl.ds(first, CH), :] - (cell_in + (m * band).astype(jnp.float32))) * scale
            offset = offset * offset
            kerns = []
            for group in range(groups):
                square = offset + dlon2[pl.ds(first, CH), group * LANES : (group + 1) * LANES]
                taper = jnp.maximum(LOG2E - square * lax.rsqrt(square), 0.0)
                twice = taper * taper
                kerns.append((twice * twice) * (1.25 * LOG2E - taper) * jnp.exp2(taper))
            kern = jnp.concatenate(kerns, axis=1)
            high_part = kern.astype(jnp.bfloat16)
            low_part = (kern - high_part.astype(jnp.float32)).astype(jnp.bfloat16)
            parts = jnp.concatenate([high_part, low_part, high_part], axis=0)
            stage[m] += jnp.dot(wts[chunk], parts, preferred_element_type=jnp.float32)
            done = chunk + 1 >= high_of(m)
            after = jnp.minimum(m + 1, bands)
            chunk = jnp.where(done, low_of(after), chunk + 1)
            chunk = jnp.where(after == bands, jnp.where(done, 0, chunk), chunk)
            m = jnp.where(done, after, m)
        return m, chunk

    first_item = (jnp.int32(0), low_of(jnp.int32(0)))
    lax.while_loop(lambda carry: carry[0] < bands, eval_items, first_item)

    part = lax.broadcasted_iota(jnp.int32, (samples, LANES), 1) // band

    def lay_out_pair(pair, carry):
        for half in range(2):
            lay_out(2 * pair + half)
        return carry

    def lay_out(block):
        at = pl.multiple_of(block * LANES, LANES)
        for group in range(groups):
            pieces = [
                stage[block * per_group + j, :, group * LANES : (group + 1) * LANES]
                for j in range(per_group)
            ]
            bit = 1
            while bit < per_group:
                keep = (part & bit) == 0
                for j in range(per_group):
                    if j & bit == 0:
                        first, second = pieces[j], pieces[j | bit]
                        pieces[j] = jnp.where(keep, first, pltpu.roll(second, bit * band, 1))
                        pieces[j | bit] = jnp.where(keep, pltpu.roll(first, LANES - bit * band, 1), second)
                bit *= 2
            for j in range(per_group):
                out_ref[group * per_group + j, :, pl.ds(at, LANES)] = pieces[j]

    lax.fori_loop(0, height // (2 * LANES), lay_out_pair, 0)


def pack_kernel(lat_hbm, lon_hbm, weights_hbm, count_ref, pack_ref, lat, sems, *, samples, slots):
    copies = [
        pltpu.make_async_copy(lat_hbm, lat, sems.at[0]),
        pltpu.make_async_copy(lon_hbm, pack_ref.at[samples + 1 : samples + 2], sems.at[1]),
        pltpu.make_async_copy(weights_hbm, pack_ref.at[0:samples], sems.at[2]),
    ]
    for copy in copies:
        copy.start()
    for copy in copies:
        copy.wait()
    slot = lax.broadcasted_iota(jnp.int32, (1, slots), 1)
    pack_ref[samples : samples + 1, :] = jnp.where(slot < count_ref[0], lat[...], FAR)


def turn_kernel(
    x_hbm, kappa_hbm, low_ref, high_ref, beta_ref, noise, kap, sem_x, sem_k, *, samples, width, height
):
    segments = height // LANES
    tall = height * samples // LANES
    copies = [pltpu.make_async_copy(x_hbm.at[:, c, :], noise.at[c], sem_x.at[c]) for c in range(width)]
    copies.append(pltpu.make_async_copy(kappa_hbm, kap, sem_k))
    for copy in copies:
        copy.start()
    copies[-1].wait()
    for column in range(width):
        half = (low_ref, high_ref)[column // PASSES]
        for i in range(segments):
            piece = kap[column : column + 1, i * LANES : (i + 1) * LANES]
            half[column % PASSES, tall + i : tall + i + 1, :] = piece
        beta_ref[column] = spread_kappa(half.at[column % PASSES], tall, samples, segments)
    for column in range(width):
        copies[column].wait()
    for column in range(width):
        half = (low_ref, high_ref)[column // PASSES]
        pieces = [noise[column, :, i * LANES : (i + 1) * LANES] for i in range(segments)]
        half[column % PASSES, 0:tall, :] = jnp.concatenate(pieces, axis=0).T


def spread_kappa(ref, start, samples, segments):
    rows = [ref[start + i : start + i + 1, :] - 0.5 for i in range(segments)]
    rows = [jnp.broadcast_to(row, (samples, LANES)) for row in rows]
    return jnp.concatenate(rows, axis=0).T


def prior_kernel(
    left_ref, low_ref, high_ref, right_ref, beta_ref, upd, out_hbm,
    noise, betas, first_y, second_y, result, sem_out, *, samples, width, height,
):
    halo = PASSES
    inner, outer = horner_coeffs()
    segments = height // LANES
    tall = height * samples // LANES
    columns = width + 2 * halo
    pitch = tall + 2 * PAD
    lane = lax.broadcasted_iota(jnp.int32, (8, LANES), 1)
    sub = lax.broadcasted_iota(jnp.int32, (8, LANES), 0)
    on_top, on_bottom = sub == 0, sub == 7
    inner_low = lane >= samples
    inner_high = lane < LANES - samples

    def at(base, offset):
        return pl.ds(pl.multiple_of(base + offset, 8), 8)

    def bring(column, carry):
        for k, ref in enumerate((left_ref, low_ref, high_ref, right_ref)):
            base = (k * halo + column) * pitch
            noise[pl.ds(pl.multiple_of(base + PAD, 8), tall), :] = ref[column, 0:tall, :]
        betas[column] = spread_kappa(left_ref.at[column], tall, samples, segments)
        betas[column + halo] = beta_ref[column]
        betas[column + 2 * halo] = beta_ref[column + halo]
        betas[column + 3 * halo] = spread_kappa(right_ref.at[column], tall, samples, segments)
        return carry

    def bring_four(four, carry):
        for k in range(4):
            bring(4 * four + k, carry)
        return carry

    lax.fori_loop(0, halo // 4, bring_four, 0)
    source = noise
    for turn in range(PASSES):
        target = (first_y, second_y)[turn % 2]
        level = PASSES - 1 - turn
        last = turn == PASSES - 1

        def sweep(column, count, source=source, target=target, level=level, last=last):
            base = column * pitch
            saved = [[] for _ in range(count)]
            for r in range(tall // 8):
                row = PAD + r * 8
                line = [source[at(base, t * pitch + row), :] for t in range(-1, count + 1)]
                for t in range(count):
                    north = source[pl.ds(base + (t * pitch + row - 1), 8), :]
                    south = source[pl.ds(base + (t * pitch + row + 1), 8), :]
                    if r == 0:
                        end = source[pl.ds(base + (t * pitch + PAD + tall - 1), 8), :]
                        end = jnp.where(inner_low, pltpu.roll(end, samples, 1), 0.0)
                        north = jnp.where(on_top, end, north)
                    if r == tall // 8 - 1:
                        end = source[pl.ds(base + (t * pitch + PAD - 7), 8), :]
                        end = jnp.where(inner_high, pltpu.roll(end, LANES - samples, 1), 0.0)
                        south = jnp.where(on_bottom, end, south)
                    beside = (north + south) + (line[t] + line[t + 2])
                    value = beside - betas[column + t, r * 8 : r * 8 + 8, :] * line[t + 1]
                    value = value + inner[level] * noise[at(base, t * pitch + row), :]
                    if last:
                        saved[t].append(value)
                    else:
                        target[at(base, t * pitch + row), :] = value
            for t in range(count if last else 0):
                own = column + t - halo
                turned = jnp.concatenate(saved[t], axis=0).T
                for i in range(segments):
                    lanes = slice(i * LANES, (i + 1) * LANES)
                    value = outer * turned[i * samples : (i + 1) * samples, :] + upd[own, :, lanes]
                    result[own, :, lanes] = value
                pltpu.make_async_copy(result.at[own], out_hbm.at[:, own, :], sem_out.at[own]).start()

        def step_wide(step, carry, sweep=sweep, turn=turn):
            sweep(turn + 1 + WIDE * step, WIDE)
            return carry

        count = columns - 2 * (turn + 1)
        lax.fori_loop(0, count // WIDE, step_wide, 0)
        if count % WIDE:
            sweep(jnp.int32(turn + 1 + count - count % WIDE), count % WIDE)
        source = target
    for column in range(width):
        pltpu.make_async_copy(result.at[column], out_hbm.at[:, column, :], sem_out.at[column]).wait()


def shift_to(value, axis, steps):
    count = lax.axis_size(axis)
    return lax.ppermute(value, axis, [(source, (source + steps) % count) for source in range(count)])


def local(white_noise, kappa_sq, station_lat, station_lon, station_weights, station_count):
    samples, width, height = white_noise.shape
    slots = station_lat.shape[0]
    halo = PASSES
    anywhere = pl.BlockSpec(memory_space=pl.ANY)
    whole = pl.BlockSpec(memory_space=pltpu.VMEM)
    hbm = pl.BlockSpec(memory_space=pltpu.HBM)

    def in_hbm(items):
        return [pltpu.with_memory_space_constraint(item, pltpu.HBM) for item in items]

    pack = pl.pallas_call(
        lambda *refs: pack_kernel(*refs, samples=samples, slots=slots),
        out_shape=pltpu.VMEM((samples + 2, slots), jnp.float32),
        in_specs=[hbm] * 3 + [pl.BlockSpec(memory_space=pltpu.SMEM)],
        out_specs=whole,
        scratch_shapes=[pltpu.VMEM((1, slots), jnp.float32), pltpu.SemaphoreType.DMA((3,))],
        compiler_params=pltpu.CompilerParams(vmem_limit_bytes=ROOM),
        name="pack",
    )(*in_hbm((station_lat[None], station_lon[None], station_weights)), station_count)
    later = lax.optimization_barrier((pack, white_noise, kappa_sq))
    pack = later[0]
    packs = []
    for step in range(-HOPS, HOPS + 1):
        packs.append(pack if step == 0 else shift_to(pack, "lon", -step))

    segments = height // LANES
    tall = height * samples // LANES
    half = pltpu.VMEM((halo, tall + segments, LANES), jnp.float32)
    low, high, beta = pl.pallas_call(
        lambda *refs: turn_kernel(*refs, samples=samples, width=width, height=height),
        out_shape=(half, half, pltpu.VMEM((width, tall, LANES), jnp.float32)),
        in_specs=[hbm] * 2,
        out_specs=(whole, whole, whole),
        scratch_shapes=[
            pltpu.VMEM((width, samples, height), jnp.float32),
            pltpu.VMEM((width, height), jnp.float32),
            pltpu.SemaphoreType.DMA((width,)),
            pltpu.SemaphoreType.DMA,
        ],
        compiler_params=pltpu.CompilerParams(vmem_limit_bytes=ROOM),
        name="turn",
    )(*in_hbm(later[1:]))
    left = shift_to(high, "lon", 1)
    right = shift_to(low, "lon", -1)
    packs = [pltpu.with_memory_space_constraint(item, pltpu.VMEM) for item in packs]

    lists = 2 * HOPS + 1
    band = HOPS * width
    bands = height // band
    rows_m = (bands + 1 + 7) // 8 * 8
    room = lists * slots + 2 * LANES
    upd = pl.pallas_call(
        lambda *refs: station_kernel(*refs, samples=samples, width=width, height=height, slots=slots),
        out_shape=pltpu.VMEM((width, samples, height), jnp.float32),
        in_specs=[whole] * lists,
        out_specs=whole,
        scratch_shapes=[
            pltpu.VMEM((8, lists * rows_m), jnp.int32),
            pltpu.SMEM((8, lists * rows_m), jnp.int32),
            pltpu.VMEM((lists, LANES, slots), jnp.bfloat16),
            pltpu.VMEM((room, LANES), jnp.float32),
            pltpu.VMEM((room, LANES), jnp.float32),
            pltpu.VMEM((room // CH, samples, 3 * CH), jnp.bfloat16),
            pltpu.VMEM((room, LANES), jnp.float32),
            pltpu.VMEM((room, band * width), jnp.float32),
            pltpu.VMEM((bands + 1, samples, band * width), jnp.float32),
            pltpu.SMEM((bands + 1,), jnp.int32),
            pltpu.SemaphoreType.DMA,
        ],
        compiler_params=pltpu.CompilerParams(vmem_limit_bytes=ROOM),
        cost_estimate=pl.CostEstimate(flops=10000000000, transcendentals=10**7, bytes_accessed=2 * 10**6),
        name="stations",
    )(*packs)
    columns = width + 2 * halo
    field = pltpu.VMEM(((columns + 2) * (tall + 2 * PAD), LANES), jnp.float32)
    fields = [left, low, high, right, beta, upd]
    fields = [pltpu.with_memory_space_constraint(item, pltpu.VMEM) for item in fields]
    return pl.pallas_call(
        lambda *refs: prior_kernel(*refs, samples=samples, width=width, height=height),
        out_shape=jax.ShapeDtypeStruct((samples, width, height), jnp.float32),
        in_specs=[whole] * 6,
        out_specs=anywhere,
        scratch_shapes=[
            field,
            pltpu.VMEM((columns + 2, tall, LANES), jnp.float32),
            field,
            field,
            pltpu.VMEM((width, samples, height), jnp.float32),
            pltpu.SemaphoreType.DMA((width,)),
        ],
        compiler_params=pltpu.CompilerParams(vmem_limit_bytes=ROOM),
        name="prior",
    )(*fields)


def solution(mesh):
    in_specs = (
        P("groups", "lon", None),
        P("lon", None),
        P(("groups", "lon")),
        P(("groups", "lon")),
        P("groups", "lon"),
        P(("groups", "lon")),
    )
    out_specs = P("groups", "lon", None)
    return jax.shard_map(local, mesh=mesh, in_specs=in_specs, out_specs=out_specs, check_vma=False)
```
